128 devices in a mesh: ctx: 32 (over y, x, core), mix: 4 (over z).
Axes of the slice: x: 4, y: 4, z: 4, core: 2. Of those that a mesh axis runs over, the one named last changes fastest.
Arguments:
- sources: float32 [16, 262144], P('mix', 'ctx'), may hold values from -6 to 6
- source_ids: int32 [8, 3], replicated, may hold values from 0 to 15
- mix_weights: float32 [8, 3], replicated, may hold values from 0.1 to 0.8, as said below
- source_lengths: int32 [8, 3], replicated, may hold values from 1024 to 8192, as said below
- w_embed: bfloat16 [512, 32], replicated, may hold values from -1 to 1
- w_qkv: bfloat16 [512, 1536], replicated, may hold values from -0.25 to 0.25
- w_out: bfloat16 [512, 512], replicated, may hold values from -0.25 to 0.25
- forget: float32 [8, 4, 8192], P('mix', None, 'ctx'), may hold values from 0.5 to 1, as said below
- cotangent: bfloat16 [8, 8192, 512], P('mix', 'ctx'), may hold values from -0.0625 to 0.0625
Outputs:
- output: bfloat16 [8, 8192, 512], P('mix', 'ctx')
- grad_qkv: float32 [512, 1536], P('ctx')
- grad_out: float32 [512, 512], P('ctx')
- grad_embed: float32 [512, 32], P('ctx')
The draws below stay inside these ranges and needn't reach their ends.
Inputs may be any that keep to these rules, and one draw needn't show every extreme that they name: `mix_weights`: each row sums to one. `source_lengths`: in every row one entry equals 8192. `forget`: below one.
All inputs are finite; a program needn't handle non-finite values.
Results may differ from the reference program's by a relative error of at most 0.015.
Values sent between devices are 32-bit elements; how exact they have to be, the bound alone decides.
A program may use at most 128 MiB of HBM per device.

```python
import math
import jax
import jax.numpy as jnp
from jax import lax

D = 512
H = 4
PATCH = 32
SPAN = 256
TERMS = 3
HEAD = 128
LENGTH = 8192
MIXTURES = 8
NSRC = 16
ROWS = 65536


def draw_mix_weights(key, part):
    draws = jax.random.uniform(jax.random.fold_in(key, 31), (MIXTURES, TERMS), minval=1e-06, maxval=1.0)
    spread = -jnp.log(draws)
    return (0.1 + 0.7 * spread / jnp.sum(spread, axis=1, keepdims=True)).astype(jnp.float32)


def draw_source_lengths(key, part):
    first_key, second_key = jax.random.split(jax.random.fold_in(key, 47))
    others = jax.random.randint(first_key, (MIXTURES, TERMS), LENGTH // 8, LENGTH + 1)
    whole = jax.random.randint(second_key, (MIXTURES,), 0, TERMS)
    slots = jnp.arange(TERMS, dtype=jnp.int32)
    return jnp.where(slots[None, :] == whole[:, None], LENGTH, others).astype(jnp.int32)


def draw_forget(key, part):
    kind_key, slow_key, fast_key, jitter_key, where_key, depth_key = jax.random.split(jax.random.fold_in(key, 59), 6)
    fast_share = 0.5
    slow_lo = 0.05
    slow_hi = 0.6
    fast = jax.random.uniform(kind_key, (MIXTURES, H, 1)) < fast_share
    slow_rate = jnp.exp(jax.random.uniform(slow_key, (MIXTURES, H, 1), minval=math.log(slow_lo / LENGTH), maxval=math.log(slow_hi / LENGTH)))
    fast_rate = jnp.exp(jax.random.uniform(fast_key, (MIXTURES, H, 1), minval=math.log(1.0 / 50.0), maxval=math.log(1.0 / 30.0)))
    rate = jnp.where(fast, fast_rate, slow_rate)
    jitter = jax.random.uniform(jitter_key, (MIXTURES, H, LENGTH), minval=0.5, maxval=1.5)
    gate_signal = jnp.minimum(1.0 - rate * jitter, 1.0 - 1.2e-07)
    spots = jax.random.randint(where_key, (MIXTURES, H, 3), 0, LENGTH)
    recursion_level = jax.random.uniform(depth_key, (MIXTURES, H, 3), minval=0.5, maxval=0.8)
    positions = jnp.arange(LENGTH, dtype=jnp.int32)
    match_flag = positions[None, None, :, None] == spots[:, :, None, :]
    spike_event = jnp.min(jnp.where(match_flag, recursion_level[:, :, None, :], 1.0), axis=-1)
    return jnp.minimum(gate_signal, spike_event).astype(jnp.float32)


def place_ends(result, own_key, smallest, top_value):
    spot = [jax.random.randint(jax.random.fold_in(own_key, axis), (), 0, length) for axis, length in enumerate(result.shape)]
    widest = result.shape.index(max(result.shape))
    neighbour = spot[:widest] + [(spot[widest] + 1) % result.shape[widest]] + spot[widest + 1:]
    return result.at[tuple(spot)].set(smallest).at[tuple(neighbour)].set(top_value)


def steps_of(stream_key, dims, cuts, least, high):
    def one(axis_at, blocks):
        heights = jax.random.uniform(jax.random.fold_in(jax.random.fold_in(stream_key, 6), axis_at), (blocks,), jnp.float32, least / len(cuts), high / len(cuts))
        return jnp.repeat(jnp.exp(heights), dims[axis_at] // blocks).reshape((-1,) + (1,) * (len(dims) - axis_at - 1))

    gain = one(*cuts[0])
    for cut in cuts[1:]:
        gain = gain * one(*cut)
    return gain


def centred(own_key, dims, scale, limit, shards=(), kind=jnp.bfloat16):
    values = jax.random.normal(own_key, dims, jnp.float32) * scale
    if len(shards) > 0:
        values = steps_of(own_key, dims, shards, -0.22, 0.18) * values
    return jnp.clip(values, min=-limit, max=limit).astype(kind)


def setup_inputs(seed: int = 0) -> dict:
    arg_keys = jax.random.split(jax.random.key(seed), 10)
    return {
        "sources": centred(arg_keys[0], (NSRC, LENGTH * PATCH), 1.0, 6.0, ((0, 4), (1, 32)), jnp.float32),
        "source_ids": place_ends(jax.random.randint(arg_keys[1], (MIXTURES, TERMS), 0, NSRC), jax.random.fold_in(arg_keys[1], 1), 0, NSRC - 1).astype(jnp.int32),
        "mix_weights": draw_mix_weights(jax.random.fold_in(arg_keys[9], 71), 0),
        "source_lengths": draw_source_lengths(jax.random.fold_in(arg_keys[9], 71), 0),
        "w_embed": centred(arg_keys[4], (D, PATCH), PATCH ** -0.5, 1.0),
        "w_qkv": centred(arg_keys[5], (D, 3 * D), D ** -0.5, 0.25),
        "w_out": centred(arg_keys[6], (D, D), D ** -0.5, 0.25),
        "forget": draw_forget(jax.random.fold_in(arg_keys[9], 71), 0),
        "cotangent": centred(arg_keys[8], (MIXTURES, LENGTH, D), (ROWS ** -0.5), 0.0625, ((0, 4), (1, 32))),
    }


EPS = 1e-06

def product(spec, left, right):
    return jnp.einsum(spec, left.astype(jnp.float32), right.astype(jnp.float32))

def scaled(array, factor):
    return (array.astype(jnp.float32) * factor[..., None]).astype(jnp.bfloat16)

def causal_decay(cumulative):
    length = cumulative.shape[-1]
    causal = jnp.arange(length)[:, None] >= jnp.arange(length)[None, :]
    return jnp.where(causal, jnp.exp(cumulative[..., :, None] - cumulative[..., None, :]), 0.0)

def block_forward(queries, key_rows, value_rows, log_gate, memory):
    cumulative = jnp.cumsum(log_gate, axis=-1)
    final = cumulative[..., -1:]
    decay_mask = causal_decay(cumulative)
    from_memory = product('bhcd,bhde->bhce', scaled(queries, jnp.exp(cumulative)), memory.astype(jnp.bfloat16))
    weights = (product('bhcd,bhsd->bhcs', queries, key_rows) * decay_mask).astype(jnp.bfloat16)
    inside = product('bhcs,bhse->bhce', weights, value_rows)
    written = product('bhcd,bhce->bhde', scaled(key_rows, jnp.exp(final - cumulative)), value_rows)
    updated = jnp.exp(final)[..., None] * memory + written
    return (from_memory + inside, updated)

def block_backward(queries, key_rows, value_rows, grad_read, log_gate, memory, later):
    cumulative = jnp.cumsum(log_gate, axis=-1)
    final = cumulative[..., -1:]
    decay_mask = causal_decay(cumulative)
    growth = jnp.exp(cumulative)
    decay_factor = jnp.exp(final - cumulative)
    left = (product('bhce,bhse->bhcs', grad_read, value_rows) * decay_mask).astype(jnp.bfloat16)
    right = (product('bhcd,bhsd->bhcs', queries, key_rows) * decay_mask).astype(jnp.bfloat16)
    later_half = later.astype(jnp.bfloat16)
    grad_query = product('bhce,bhde->bhcd', scaled(grad_read, growth), memory.astype(jnp.bfloat16)) + product('bhcs,bhsd->bhcd', left, key_rows)
    grad_key = product('bhcs,bhcd->bhsd', left, queries) + product('bhse,bhde->bhsd', scaled(value_rows, decay_factor), later_half)
    grad_value = product('bhcs,bhce->bhse', right, grad_read) + product('bhsd,bhde->bhse', scaled(key_rows, decay_factor), later_half)
    earlier = jnp.exp(final)[..., None] * later + product('bhcd,bhce->bhde', scaled(queries, growth), grad_read)
    return (grad_query, grad_key, grad_value, earlier)

def to_blocks(array):
    shaped = array.reshape(array.shape[:2] + (array.shape[2] // SPAN, SPAN) + array.shape[3:])
    return jnp.moveaxis(shaped, 2, 0)

def from_blocks(blocked):
    moved = jnp.moveaxis(blocked, 0, 2)
    return moved.reshape(moved.shape[:2] + (moved.shape[2] * moved.shape[3],) + moved.shape[4:])

def reference(sources, source_ids, mix_weights, source_lengths, w_embed, w_qkv, w_out, forget, cotangent):
    positions = jnp.arange(LENGTH, dtype=jnp.int32)
    mixture = jnp.zeros((MIXTURES, LENGTH, PATCH), jnp.float32)
    for term in range(TERMS):
        chosen = sources[source_ids[:, term]].reshape(MIXTURES, LENGTH, PATCH)
        cover = jnp.where(positions[None, :] < source_lengths[:, term:term + 1], mix_weights[:, term:term + 1], 0.0)
        mixture = mixture + cover[:, :, None] * chosen

    def one_mixture(inputs):
        mixture_one, forget_one, cotangent_one = inputs
        mixture_half = mixture_one.astype(jnp.bfloat16)
        embedded = jnp.dot(mixture_half, w_embed.T, preferred_element_type=jnp.float32).astype(jnp.bfloat16)
        projected = jnp.dot(embedded, w_qkv, preferred_element_type=jnp.float32).astype(jnp.bfloat16)
        parts = projected.reshape(LENGTH, 3, H, HEAD).transpose(1, 2, 0, 3)
        queries = parts[0][None]
        key_rows = parts[1][None]
        value_rows = parts[2][None]
        log_gate = jnp.log1p(forget_one - 1.0)[None]
        query_blocks = to_blocks(queries)
        key_blocks = to_blocks(key_rows)
        value_blocks = to_blocks(value_rows)
        gate_blocks = to_blocks(log_gate)

        def forward_step(memory, inputs_block):
            read_block, updated = block_forward(inputs_block[0], inputs_block[1], inputs_block[2], inputs_block[3], memory)
            return (updated, (read_block, memory))
        start = jnp.zeros((1, H, HEAD, HEAD), jnp.float32)
        last_state, (read_blocks, block_states) = lax.scan(forward_step, start, (query_blocks, key_blocks, value_blocks, gate_blocks))
        read = from_blocks(read_blocks)
        inverse_rms = lax.rsqrt(lax.optimization_barrier(jnp.mean(read * read, axis=-1, keepdims=True)) + EPS)
        normed = read * inverse_rms
        normed_half = normed[0].transpose(1, 0, 2).reshape(LENGTH, D).astype(jnp.bfloat16)
        output_one = jnp.dot(normed_half, w_out, preferred_element_type=jnp.float32).astype(jnp.bfloat16)
        grad_out_one = jnp.dot(normed_half.T, cotangent_one, preferred_element_type=jnp.float32)
        grad_normed = jnp.dot(cotangent_one, w_out.T, preferred_element_type=jnp.float32)
        grad_normed = grad_normed.reshape(LENGTH, H, HEAD).transpose(1, 0, 2)[None]
        grad_read = (inverse_rms * (grad_normed - normed * lax.optimization_barrier(jnp.mean(grad_normed * normed, axis=-1, keepdims=True)))).astype(jnp.bfloat16)

        def backward_step(later, inputs_block):
            grad_query, grad_key, grad_value, earlier = block_backward(inputs_block[0], inputs_block[1], inputs_block[2], inputs_block[3], inputs_block[4], inputs_block[5], later)
            return (earlier, (grad_query, grad_key, grad_value))
        first_back, (query_grads, key_grads, value_grads) = lax.scan(backward_step, start, (query_blocks, key_blocks, value_blocks, to_blocks(grad_read), gate_blocks, block_states), reverse=True)
        stacked = jnp.stack([from_blocks(query_grads)[0], from_blocks(key_grads)[0], from_blocks(value_grads)[0]])
        grad_proj = stacked.transpose(2, 0, 1, 3).reshape(LENGTH, 3 * D).astype(jnp.bfloat16)
        grad_qkv_one = jnp.dot(embedded.T, grad_proj, preferred_element_type=jnp.float32)
        grad_embedded = jnp.dot(grad_proj, w_qkv.T, preferred_element_type=jnp.float32).astype(jnp.bfloat16)
        grad_embed_one = jnp.dot(grad_embedded.T, mixture_half, preferred_element_type=jnp.float32)
        return (output_one, grad_qkv_one, grad_out_one, grad_embed_one)
    outputs, grad_qkv_all, grad_out_all, grad_embed_all = lax.map(one_mixture, (mixture, forget, cotangent))
    return (outputs, lax.optimization_barrier(jnp.sum(grad_qkv_all, axis=0)), lax.optimization_barrier(jnp.sum(grad_out_all, axis=0)), lax.optimization_barrier(jnp.sum(grad_embed_all, axis=0)))
```

```python
import jax
import jax.numpy as jnp
from jax import lax
from jax.sharding import PartitionSpec as P

EPS = 1e-06
BF = jnp.bfloat16
F32 = jnp.float32


def mm(left, right, dims):
    return lax.dot_general(left.astype(BF), right.astype(BF), (dims, ((), ())), preferred_element_type=F32)


def shards(
    sources, source_ids, mix_weights, source_lengths, w_embed, w_qkv, w_out, forget, cotangent
):
    mix_index = lax.axis_index("mix")
    ctx_index = lax.axis_index("ctx")
    patch = w_embed.shape[1]
    local_sources = sources.shape[0]
    steps = sources.shape[1] // patch
    local_mix, heads = forget.shape[0], forget.shape[1]
    width = w_out.shape[0]
    head = width // heads
    lanes = heads * patch
    positions = ctx_index * steps + jnp.arange(steps, dtype=jnp.int32)
    own = mix_index * local_sources + jnp.arange(local_sources, dtype=jnp.int32)
    series = sources.reshape(local_sources, steps, patch)
    cover = jnp.where(positions[None, None, :] < source_lengths[:, :, None], mix_weights[:, :, None], 0.0)
    part = 0.0
    for s in range(local_sources):
        amount = jnp.sum(jnp.where((source_ids == own[s])[:, :, None], cover, 0.0), axis=1)
        part = part + amount[:, :, None] * series[s][None]
    mixture = lax.optimization_barrier(
        lax.psum_scatter(part, "mix", scatter_dimension=0, tiled=True)
    )
    m = mixture.astype(BF)

    wt = mm(w_embed, w_qkv, ((0,), (0,)))
    stack = lambda j: wt[:, j * width : (j + 1) * width].reshape(patch, heads, head).transpose(1, 0, 2).astype(BF)
    at, bt, ct = stack(0), stack(1), stack(2)
    gram = jnp.einsum("hid,hjd->hij", at, bt, preferred_element_type=F32).astype(BF)
    wo = jnp.einsum("hid,hdo->hio", ct, w_out.reshape(heads, head, width), preferred_element_type=F32).astype(BF)
    kk = jnp.einsum("hid,hjd->hij", ct, ct, preferred_element_type=F32).astype(BF)

    log_gate = jnp.log1p(forget - 1.0)
    g = jnp.cumsum(log_gate, axis=-1)
    last = g[..., -1:]
    causal = jnp.arange(steps)[:, None] >= jnp.arange(steps)[None, :]
    decay = jnp.where(causal, jnp.exp(g[..., :, None] - g[..., None, :]), 0.0)
    me = (m.astype(F32)[:, None] * jnp.exp(last - g)[..., None]).astype(BF)
    local = jnp.einsum("bti,bhtj->bhij", m, me, preferred_element_type=F32)
    packed = jnp.concatenate([local.reshape(-1), last.reshape(-1)])
    gathered = lax.all_gather(packed, "ctx")
    count = gathered.shape[0]
    ends = gathered[:, : local.size].reshape((count,) + local.shape)
    lasts = gathered[:, local.size :].reshape(count, local_mix, heads)
    before = jnp.cumsum(lasts, axis=0) - 0.0
    mine = lax.dynamic_index_in_dim(before - lasts, ctx_index, 0, True)
    earlier = (jnp.arange(count) < ctx_index)[:, None, None]
    factor = jnp.where(earlier, jnp.exp(jnp.where(earlier, mine - before, 0.0)), 0.0)
    memory = jnp.sum(factor[..., None, None] * ends, axis=0).astype(BF)

    mg = jnp.einsum("bti,hij->bhtj", m, gram, preferred_element_type=F32).astype(BF)
    scores = (jnp.einsum("bhtj,bsj->bhts", mg, m, preferred_element_type=F32) * decay).astype(BF)
    growth = jnp.exp(g)[..., None]
    mge = (mg.astype(F32) * growth).astype(BF)
    u = jnp.einsum("bhts,bsi->bhti", scores, m, preferred_element_type=F32) + jnp.einsum(
        "bhtj,bhji->bhti", mge, memory, preferred_element_type=F32
    )
    uh = u.astype(BF)
    read = jnp.einsum("bhti,hid->bhtd", uh, ct, preferred_element_type=F32)
    inv = lax.rsqrt(jnp.mean(read * read, axis=-1, keepdims=True) + EPS)
    n = (u * inv).astype(BF)
    output = jnp.einsum("bhti,hio->bto", n, wo, preferred_element_type=F32).astype(BF)
    y0 = jnp.einsum("bto,hio->bhti", cotangent, wo, preferred_element_type=F32)
    ku = jnp.einsum("bhti,hij->bhtj", uh, kk, preferred_element_type=F32)
    mu = inv * jnp.sum(y0 * u, axis=-1, keepdims=True) / head
    y = inv * (y0 - inv * mu * ku)
    yh = y.astype(BF)
    left = (jnp.einsum("bhtj,bsj->bhts", yh, m, preferred_element_type=F32) * decay).astype(BF)
    a = jnp.einsum("bhts,bsi->bhti", left, m, preferred_element_type=F32) + jnp.einsum(
        "bhtj,bhji->bhti", (y * growth).astype(BF), memory, preferred_element_type=F32
    )
    x = jnp.einsum("bti,bhtj->hij", m, a.astype(BF), preferred_element_type=F32)
    z = jnp.einsum("bhti,bto->hio", n, cotangent, preferred_element_type=F32)
    v = jnp.einsum("bhti,bhtj->hij", (u * inv * mu).astype(BF), n, preferred_element_type=F32)
    x, z, v = lax.optimization_barrier(lax.psum((x, z, v), ("ctx", "mix")))
    exact = lambda spec, left, right: jnp.einsum(
        spec, left, right.astype(F32), precision=lax.Precision.HIGHEST, preferred_element_type=F32
    )
    yq = exact("hij,hjd->hid", x, bt)
    yk = exact("hji,hjd->hid", x, at)
    yv = exact("hio,hdo->hid", z, w_out.reshape(heads, head, width)) - exact("hij,hjd->hid", v, ct)
    ys = jnp.concatenate([q.transpose(1, 0, 2).reshape(patch, width) for q in (yq, yk, yv)], axis=1)
    rows = width // count
    we = lax.dynamic_slice_in_dim(w_embed, ctx_index * rows, rows, 0)
    wq = lax.dynamic_slice_in_dim(w_qkv, ctx_index * rows, rows, 0)
    grad_qkv = mm(we, ys, ((1,), (0,)))
    grad_embed = mm(wq, ys, ((1,), (1,)))
    full = exact("hio,hid->hdo", z, ct).reshape(width, width)
    grad_out = lax.dynamic_slice_in_dim(full, ctx_index * rows, rows, 0)
    return (output, grad_qkv, grad_out, grad_embed)


def solution(mesh):
    placed = (
        P("mix", "ctx"),
        P(),
        P(),
        P(),
        P(),
        P(),
        P(),
        P("mix", None, "ctx"),
        P("mix", "ctx", None),
    )
    return jax.shard_map(
        shards,
        mesh=mesh,
        in_specs=placed,
        out_specs=(P("mix", "ctx", None), P("ctx", None), P("ctx", None), P("ctx", None)),
        check_vma=False,
    )
```

```python
import jax
import jax.numpy as jnp
from jax import lax
from jax.experimental import pallas as pl
from jax.experimental.pallas import tpu as pltpu
from jax.sharding import PartitionSpec as P

EPS = 1e-06
BF = jnp.bfloat16
F32 = jnp.float32
MESH = pl.DeviceIdType.MESH
NCTX = 32
NMIX = 4
NDEV = 128
LB = 2
HEADS = 4
PATCH = 32
STEPS = 256
ROWS = LB * STEPS
HEAD = 128
WIDTH = 512
LOCAL_SOURCES = 4
TERMS = 3
VX = WIDTH + HEAD


def mm(left, right, dims=((1,), (0,))):
    return lax.dot_general(left, right, (dims, ((), ())), preferred_element_type=F32)


NT = ((1,), (1,))
TN = ((0,), (0,))


def mm_exact(left, right, dims):
    return lax.dot_general(
        left, right, (dims, ((), ())), precision=lax.Precision.HIGHEST, preferred_element_type=F32
    )


def iota(shape, axis):
    return lax.broadcasted_iota(jnp.int32, shape, axis)


def kernel(
    src_hbm, ids_hbm, wts_hbm, lens_hbm, we_hbm, wq_hbm, wo_hbm, forget_hbm, cot_hbm,
    out_hbm, gqkv_hbm, gout_hbm, gemb_hbm,
    src, ids, wts, lens, we, wq, wo, forget, cot,
    stage_mix, recv_mix, glast, recv_g, m_local, recv_m, stage_s, recv_s,
    decay, m4, mgs, u_ref, a_ref, y_ref, gcol, at, bt, ct, ctbig, gram, kk, wop, y0,
    zall, recv_z, zrow, recv_zh, yxrow, recv_yx,
    out, gqkv, gout, gemb, spare_g, spare_m, spare_s, spare_z, spare_yx, spare_zh,
    in_sem, mix_s, mix_r, g_s, g_r, m_s, m_r, s_s, s_r, z_s, z_r, zh_s, zh_r, yx_s, yx_r, out_sem,
):
    ctx = lax.axis_index("ctx")
    mix = lax.axis_index("mix")
    me = ctx * NMIX + mix
    plane = ctx // 8

    moves = [
        (ids_hbm, ids), (wts_hbm, wts), (lens_hbm, lens), (forget_hbm, forget),
        (we_hbm, we), (wq_hbm, wq), (wo_hbm, wo), (cot_hbm, cot),
    ] + [(src_hbm.at[:, s], src.at[s]) for s in range(LOCAL_SOURCES)]
    loads = [pltpu.make_async_copy(a, b, in_sem.at[i]) for i, (a, b) in enumerate(moves)]
    for i in (8, 9, 10, 11, 0, 1, 2, 3, 4, 5, 6, 7):
        loads[i].start()

    def device(flat):
        return (flat // NMIX, lax.rem(flat, NMIX))

    barrier = pltpu.get_barrier_semaphore()

    def greet(o, carry):
        pl.semaphore_signal(
            barrier, inc=1, device_id=device(lax.rem(me + o, NDEV)), device_id_type=MESH
        )
        return carry

    lax.fori_loop(1, NDEV, greet, 0)

    for load in loads[:3] + loads[8:]:
        load.wait()
    place = ctx * STEPS + 4 * iota((64, 128), 0) + iota((64, 128), 1) // PATCH
    for b in range(LB * NMIX):
        part = jnp.zeros((64, 128), F32)
        for j in range(TERMS):
            slot = ids[j, b] - mix * LOCAL_SOURCES
            held = jnp.clip(slot, 0, LOCAL_SOURCES - 1)
            weight = jnp.where(slot == held, wts[j, b], 0.0)
            part = part + jnp.where(place < lens[j, b], weight, 0.0) * src[held]
        stage_mix[b] = part

    loads[3].wait()
    tri = (iota((STEPS, STEPS), 0) >= iota((STEPS, STEPS), 1)).astype(F32)
    growth = []
    for b in range(LB):
        gate = jnp.log1p(forget[b] - 1.0)
        wide = jnp.concatenate(
            [jnp.broadcast_to(gate[h : h + 1], (PATCH, STEPS)) for h in range(HEADS)], axis=0
        )
        col = mm_exact(tri, wide, NT)
        gcol[b] = col
        glast[b : b + 1] = col[STEPS - 1 : STEPS]
        growth.append(mm_exact(gate, tri, NT))

    pl.semaphore_wait(barrier, NDEV - 1)

    own_mix = pltpu.make_async_copy(stage_mix.at[pl.ds(LB * mix, LB)], recv_mix.at[mix], mix_r)
    own_mix.start()
    for o in range(1, NMIX):
        other = lax.rem(mix + o, NMIX)
        pltpu.make_async_remote_copy(
            stage_mix.at[pl.ds(LB * other, LB)], recv_mix.at[mix], mix_s, mix_r,
            device_id=(ctx, other), device_id_type=MESH,
        ).start()

    def spare_copy(part, spare, send):
        pltpu.make_async_copy(part, spare, send).start()

    def ctx_rows(spare, src_ref, dst_ref, send, recv, src_row, dst_row):
        def one(o, carry):
            other = lax.rem(ctx + o, NCTX)
            pltpu.make_async_remote_copy(
                src_ref.at[pl.ds(src_row(other), 2)], dst_ref.at[pl.ds(dst_row, 2)], send, recv,
                device_id=(other, mix), device_id_type=MESH,
            ).start()
            return carry

        lax.fori_loop(1, NCTX, one, 0)
        spare_copy(src_ref.at[pl.ds(src_row(ctx), 2)], spare, send)
        pltpu.make_async_copy(
            src_ref.at[pl.ds(src_row(ctx), 2)], dst_ref.at[pl.ds(dst_row, 2)], recv
        ).start()

    ctx_rows(spare_g, glast, recv_g, g_s, g_r, lambda other: 0, 2 * ctx)

    for load in loads[4:7]:
        load.wait()
    wt = mm(we[...], wq[...]).astype(BF)
    lane = iota((1, HEAD), 1)
    block = iota((HEAD, HEAD), 0) // PATCH == iota((HEAD, HEAD), 1) // PATCH
    heads = [lane // PATCH == h for h in range(HEADS)]
    for h in range(HEADS):
        rows = pl.ds(h * PATCH, PATCH)
        at[rows] = wt[:, h * HEAD : (h + 1) * HEAD]
        bt[rows] = wt[:, WIDTH + h * HEAD : WIDTH + (h + 1) * HEAD]
        piece = wt[:, 2 * WIDTH + h * HEAD : 2 * WIDTH + (h + 1) * HEAD]
        ct[rows] = piece
        for k in range(HEADS):
            ctbig[rows, k * HEAD : (k + 1) * HEAD] = piece if k == h else jnp.zeros_like(piece)
    gram[...] = jnp.where(block, mm(at[...], bt[...], NT), 0.0).astype(BF)
    kk[...] = jnp.where(block, mm(ct[...], ct[...], NT), 0.0).astype(BF)
    wop[...] = mm(ctbig[...], wo[...]).astype(BF)
    loads[7].wait()
    y0[...] = mm(cot[...], wop[...], NT)

    causal = iota((STEPS, STEPS), 0) >= iota((STEPS, STEPS), 1)
    for b in range(LB):
        for h in range(HEADS):
            diff = gcol[b][:, h * PATCH : h * PATCH + 1] - growth[b][h : h + 1]
            decay[b * HEADS + h] = jnp.where(causal, jnp.exp(diff), 0.0)

    pltpu.make_async_copy(recv_mix, recv_mix, mix_r).wait()
    spread = (lax.rem(iota((HEAD, HEAD), 0), PATCH) == lax.rem(iota((HEAD, HEAD), 1), PATCH)).astype(BF)
    pick = (iota((STEPS, 64), 0) // 4 == iota((STEPS, 64), 1)).astype(BF)
    mine = lax.rem(iota((STEPS, HEAD), 0), 4) == iota((STEPS, HEAD), 1) // PATCH
    for b in range(LB):
        packed = ((recv_mix[0, b] + recv_mix[1, b]) + (recv_mix[2, b] + recv_mix[3, b])).astype(BF)
        lone = jnp.where(mine, mm(pick, packed), 0.0).astype(BF)
        rows = mm(lone, spread)
        m4[pl.ds(b * STEPS, STEPS)] = rows.astype(BF)
        faded = (rows * jnp.exp(glast[b : b + 1] - gcol[b])).astype(BF)
        m_local[pl.ds(b * PATCH, PATCH)] = mm(rows.astype(BF), faded, TN)[:PATCH]
    ctx_rows(spare_m, m_local, recv_m, m_s, m_r, lambda other: 2 * other, 2 * ctx)

    for b in range(LB):
        rows = pl.ds(b * STEPS, STEPS)
        mb = m4[rows]
        mg = mm(mb, gram[...])
        mgs[rows] = (mg * jnp.exp(gcol[b])).astype(BF)
        mgb = mg.astype(BF)
        total = jnp.zeros((STEPS, HEAD), F32)
        for h in range(HEADS):
            score = mm(jnp.where(heads[h], mgb, jnp.zeros_like(mgb)), mb, NT)
            score = (score * decay[b * HEADS + h]).astype(BF)
            total = total + mm(score, jnp.where(heads[h], mb, jnp.zeros_like(mb)))
        u_ref[rows] = total

    pltpu.make_async_copy(recv_g, recv_g, g_r).wait()
    pltpu.make_async_copy(recv_m, recv_m, m_r).wait()
    own_b = ctx // (NCTX // LB)
    state = jnp.zeros((2, HEAD), F32)
    for j in range(NCTX):
        stage_s[2 * j : 2 * j + 2] = state
        state = jnp.exp(recv_g[pl.ds(2 * j + own_b, 1)]) * state + recv_m[2 * j : 2 * j + 2]
    ctx_rows(spare_s, stage_s, recv_s, s_s, s_r, lambda other: 2 * other, 2 * ctx)
    pltpu.make_async_copy(recv_s, recv_s, s_r).wait()

    memory = []
    for b in range(LB):
        part = recv_s[pl.ds(b * PATCH, PATCH)]
        memory.append(
            jnp.where(block, jnp.concatenate([part] * HEADS, axis=0), 0.0).astype(BF)
        )
        rows = pl.ds(b * STEPS, STEPS)
        u_ref[rows] = u_ref[rows] + mm(mgs[rows], memory[b])
    u = u_ref[...]
    ub = u.astype(BF)
    read = mm(ub, ctbig[...])
    sums = (iota((WIDTH, HEAD), 0) // HEAD == iota((WIDTH, HEAD), 1) // PATCH).astype(BF)
    square = mm((read * read).astype(BF), sums) * (1.0 / HEAD)
    inv = lax.rsqrt(square + EPS)
    n = u * inv
    nb = n.astype(BF)
    dots = mm((y0[...] * u).astype(BF), block.astype(BF)) * (1.0 / HEAD)
    drift = inv * (inv * dots)
    y = inv * (y0[...] - drift * mm(ub, kk[...]))
    y_ref[...] = y
    for b in range(LB):
        rows = pl.ds(b * STEPS, STEPS)
        mb = m4[rows]
        yb = y_ref[rows]
        yh = yb.astype(BF)
        total = mm((yb * jnp.exp(gcol[b])).astype(BF), memory[b])
        for h in range(HEADS):
            left = mm(jnp.where(heads[h], yh, jnp.zeros_like(yh)), mb, NT)
            left = (left * decay[b * HEADS + h]).astype(BF)
            total = total + mm(left, jnp.where(heads[h], mb, jnp.zeros_like(mb)))
        a_ref[rows] = total.astype(BF)

    def repeat(square_block):
        kept = jnp.where(block, square_block, 0.0)
        kept = kept + pltpu.roll(kept, 64, 1)
        return kept + pltpu.roll(kept, 32, 1)

    zall[:, :WIDTH] = mm(nb, cot[...], TN)
    v_rows = repeat(mm((n * (inv * dots)).astype(BF), nb, TN))
    x_rows = repeat(mm(m4[...], a_ref[...], TN))
    zall[:, WIDTH:] = jnp.where(lane < 64, v_rows, x_rows)

    def scatter(o, carry):
        other = lax.rem(me + o, NDEV)
        pltpu.make_async_remote_copy(
            zall.at[pl.ds(other, 1)], recv_z.at[pl.ds(me, 1)], z_s, z_r,
            device_id=device(other), device_id_type=MESH,
        ).start()
        return carry

    lax.fori_loop(1, NDEV, scatter, 0)
    spare_copy(zall.at[pl.ds(me, 1)], spare_z, z_s)
    pltpu.make_async_copy(zall.at[pl.ds(me, 1)], recv_z.at[pl.ds(me, 1)], z_r).start()

    out[...] = mm(nb, wop[...]).astype(BF)
    store_out = pltpu.make_async_copy(out, out_hbm, out_sem.at[0])
    store_out.start()

    pltpu.make_async_copy(recv_z, recv_z, z_r).wait()
    row = jnp.sum(recv_z[...], axis=0, keepdims=True)
    zrow[...] = row[:, :WIDTH]
    mixed = row[:, WIDTH:]
    fine = row[:, :WIDTH]
    high = fine.astype(BF)
    low = (fine - high.astype(F32)).astype(BF)
    w_head = wo[pl.ds(plane * HEAD, HEAD)]
    c_head = ct[pl.ds(plane * PATCH, PATCH)]
    yv = mm(high, w_head, NT) + mm(low, w_head, NT) - mm(mixed[:, :PATCH].astype(BF), c_head)
    xs = jnp.where(lane < 64, 0.0, mixed)
    yxrow[:, :HEAD] = yv
    yxrow[:, HEAD:] = xs + pltpu.roll(xs, 64, 1)

    def spread_row(o, carry):
        pltpu.make_async_remote_copy(
            yxrow, recv_yx.at[pl.ds(me, 1)], yx_s, yx_r,
            device_id=device(lax.rem(me + o, NDEV)), device_id_type=MESH,
        ).start()
        return carry

    lax.fori_loop(1, NDEV, spread_row, 0)
    spare_copy(yxrow, spare_yx, yx_s)
    pltpu.make_async_copy(yxrow, recv_yx.at[pl.ds(me, 1)], yx_r).start()
    local = lax.rem(me, NCTX)

    def spread_z(o, carry):
        pltpu.make_async_remote_copy(
            zrow, recv_zh.at[pl.ds(local, 1)], zh_s, zh_r,
            device_id=device(plane * NCTX + lax.rem(local + o, NCTX)), device_id_type=MESH,
        ).start()
        return carry

    lax.fori_loop(1, NCTX, spread_z, 0)
    spare_copy(zrow, spare_zh, zh_s)
    pltpu.make_async_copy(zrow, recv_zh.at[pl.ds(local, 1)], zh_r).start()

    chosen = (iota((16, HEAD), 1) == 16 * lax.rem(ctx, 8) + iota((16, HEAD), 0)).astype(BF)
    c_rows = mm(chosen, c_head, NT).astype(BF)
    column = (iota((16, WIDTH), 1) == ctx * 16 + iota((16, WIDTH), 0)).astype(BF)
    embed_rows = mm(column, jnp.concatenate([we[...]] * HEADS, axis=0), NT).astype(BF)
    tall = jnp.concatenate([jnp.where(heads[h], embed_rows, jnp.zeros_like(embed_rows)) for h in range(HEADS)], axis=0)
    qkv_rows = wq[pl.ds(ctx * 16, 16)]
    long = jnp.concatenate(
        [
            jnp.concatenate(
                [qkv_rows[:, j * WIDTH + h * HEAD : j * WIDTH + (h + 1) * HEAD] for j in range(3)], axis=1
            )
            for h in range(HEADS)
        ],
        axis=0,
    )

    pltpu.make_async_copy(recv_yx, recv_yx, yx_r).wait()
    x_block = jnp.where(block, recv_yx[:, HEAD:], 0.0).astype(BF)
    yq = mm(x_block, bt[...])
    yk = mm(x_block, at[...], TN)
    ys = jnp.concatenate([yq, yk, recv_yx[:, :HEAD]], axis=1).astype(BF)
    wide = mm(tall, ys)
    for h in range(HEADS):
        for j in range(3):
            gqkv[:, j * WIDTH + h * HEAD : j * WIDTH + (h + 1) * HEAD] = wide[
                16 * h : 16 * h + 16, j * HEAD : (j + 1) * HEAD
            ]
    tops = mm(long, ys, NT)
    folded = jnp.zeros((16, HEAD), F32)
    for h in range(HEADS):
        folded = folded + jnp.where(heads[h], tops[16 * h : 16 * h + 16], 0.0)
    folded = folded + pltpu.roll(folded, 64, 1)
    folded = folded + pltpu.roll(folded, 32, 1)
    gemb[...] = folded[:, :PATCH]
    store_qkv = pltpu.make_async_copy(gqkv, gqkv_hbm, out_sem.at[1])
    store_qkv.start()
    store_emb = pltpu.make_async_copy(gemb, gemb_hbm, out_sem.at[2])
    store_emb.start()
    pltpu.make_async_copy(recv_zh, recv_zh, zh_r).wait()
    gout[...] = mm(c_rows, recv_zh[...].astype(BF))
    store_gout = pltpu.make_async_copy(gout, gout_hbm, out_sem.at[3])
    store_gout.start()

    sent_mix = stage_mix.at[pl.ds(0, LB * (NMIX - 1))]
    pltpu.make_async_copy(sent_mix, sent_mix, mix_s).wait()
    for ref, sem in (
        (recv_g, g_s), (recv_m, m_s), (recv_s, s_s), (recv_z, z_s), (recv_yx, yx_s), (recv_zh, zh_s)
    ):
        pltpu.make_async_copy(ref, ref, sem).wait()
    for store in (store_out, store_qkv, store_emb, store_gout):
        store.wait()


def hand_on(*refs):
    source, target, held, (come, go) = refs[:4], refs[4:8], refs[8:12], refs[12:]
    pieces = [pl.ds(i * STEPS // 2, STEPS // 2) for i in range(2 * LB)]
    moves = [(source[0].at[p], held[0].at[p], target[0].at[p]) for p in pieces]
    moves += [(source[i], held[i], target[i]) for i in range(1, 4)]
    arrive = [pltpu.make_async_copy(a, b, come.at[i]) for i, (a, b, c) in enumerate(moves)]
    leave = [pltpu.make_async_copy(b, c, go.at[i]) for i, (a, b, c) in enumerate(moves)]
    for copy in arrive:
        copy.start()
    for copy, after in zip(arrive, leave):
        copy.wait()
        after.start()
    for copy in leave:
        copy.wait()


def shards(
    sources, source_ids, mix_weights, source_lengths, w_embed, w_qkv, w_out, forget, cotangent
):
    packed = sources.reshape(LOCAL_SOURCES, STEPS * PATCH // 128, 128).transpose(1, 0, 2)
    vm = pltpu.VMEM
    sm = pltpu.SMEM
    dma = pltpu.SemaphoreType.DMA
    results = pl.pallas_call(
        kernel,
        out_shape=(
            jax.ShapeDtypeStruct((ROWS, WIDTH), BF),
            jax.ShapeDtypeStruct((16, 3 * WIDTH), F32),
            jax.ShapeDtypeStruct((16, WIDTH), F32),
            jax.ShapeDtypeStruct((16, PATCH), F32),
        ),
        in_specs=[pl.BlockSpec(memory_space=pl.ANY)] * 9,
        out_specs=(pl.BlockSpec(memory_space=pl.ANY),) * 4,
        scratch_shapes=[
            vm((LOCAL_SOURCES, 64, 128), F32),
            sm((TERMS, LB * NMIX), jnp.int32),
            sm((TERMS, LB * NMIX), F32),
            sm((TERMS, LB * NMIX), jnp.int32),
            vm((PATCH, WIDTH), BF),
            vm((WIDTH, 3 * WIDTH), BF),
            vm((WIDTH, WIDTH), BF),
            vm((LB, HEADS, STEPS), F32),
            vm((ROWS, WIDTH), BF),
            vm((LB * NMIX, 64, 128), F32),
            vm((NMIX, LB, 64, 128), F32),
            vm((LB, HEAD), F32),
            vm((2 * NCTX, HEAD), F32),
            vm((2 * NCTX, HEAD), F32),
            vm((2 * NCTX, HEAD), F32),
            vm((2 * NCTX, HEAD), F32),
            vm((2 * NCTX, HEAD), F32),
            vm((LB * HEADS, STEPS, STEPS), F32),
            vm((ROWS, HEAD), BF),
            vm((ROWS, HEAD), BF),
            vm((ROWS, HEAD), F32),
            vm((ROWS, HEAD), BF),
            vm((ROWS, HEAD), F32),
            vm((LB, STEPS, HEAD), F32),
            vm((HEAD, HEAD), BF),
            vm((HEAD, HEAD), BF),
            vm((HEAD, HEAD), BF),
            vm((HEAD, WIDTH), BF),
            vm((HEAD, HEAD), BF),
            vm((HEAD, HEAD), BF),
            vm((HEAD, WIDTH), BF),
            vm((ROWS, HEAD), F32),
            vm((NDEV, VX), F32),
            vm((NDEV, VX), F32),
            vm((1, WIDTH), F32),
            vm((NCTX, WIDTH), F32),
            vm((1, 2 * HEAD), F32),
            vm((NDEV, 2 * HEAD), F32),
            vm((ROWS, WIDTH), BF),
            vm((16, 3 * WIDTH), F32),
            vm((16, WIDTH), F32),
            vm((16, PATCH), F32),
            vm((2, HEAD), F32),
            vm((2, HEAD), F32),
            vm((2, HEAD), F32),
            vm((1, VX), F32),
            vm((1, 2 * HEAD), F32),
            vm((1, WIDTH), F32),
            dma((12,)),
        ]
        + [dma(())] * 14
        + [dma((4,))],
        compiler_params=pltpu.CompilerParams(collective_id=0, has_side_effects=True, vmem_limit_bytes=60 << 20),
        name="whole_step",
    )(
        packed, source_ids.T, mix_weights.T, source_lengths.T, w_embed.T, w_qkv, w_out, forget,
        cotangent.reshape(ROWS, WIDTH),
    )
    output, grad_qkv, grad_out, grad_embed = pl.pallas_call(
        hand_on,
        out_shape=tuple(jax.ShapeDtypeStruct(r.shape, r.dtype) for r in results),
        in_specs=[pl.BlockSpec(memory_space=pl.ANY)] * 4,
        out_specs=(pl.BlockSpec(memory_space=pl.ANY),) * 4,
        scratch_shapes=[vm(r.shape, r.dtype) for r in results] + [dma((8,)), dma((8,))],
        name="hand_on",
    )(*results)
    return (output.reshape(LB, STEPS, WIDTH), grad_qkv, grad_out, grad_embed)


def solution(mesh):
    placed = (
        P("mix", "ctx"),
        P(),
        P(),
        P(),
        P(),
        P(),
        P(),
        P("mix", None, "ctx"),
        P("mix", "ctx", None),
    )
    return jax.shard_map(
        shards,
        mesh=mesh,
        in_specs=placed,
        out_specs=(P("mix", "ctx", None), P("ctx", None), P("ctx", None), P("ctx", None)),
        check_vma=False,
    )
```

```python
import jax
import jax.numpy as jnp
from jax import lax
from jax.experimental import pallas as pl
from jax.experimental.pallas import tpu as pltpu
from jax.sharding import PartitionSpec as P

EPS = 1e-06
BF = jnp.bfloat16
F32 = jnp.float32
MESH = pl.DeviceIdType.MESH
NCTX = 32
NMIX = 4
NDEV = 128
LB = 2
HEADS = 4
PATCH = 32
STEPS = 256
ROWS = LB * STEPS
HEAD = 128
WIDTH = 512
LOCAL_SOURCES = 4
TERMS = 3
VX = WIDTH + HEAD
RESULTS = (((ROWS, WIDTH), BF), ((16, 3 * WIDTH), F32), ((16, WIDTH), F32), ((16, PATCH), F32))


def mm(left, right, dims=((1,), (0,))):
    return lax.dot_general(left, right, (dims, ((), ())), preferred_element_type=F32)


NT = ((1,), (1,))
TN = ((0,), (0,))


def mm_exact(left, right, dims):
    return lax.dot_general(
        left, right, (dims, ((), ())), precision=lax.Precision.HIGHEST, preferred_element_type=F32
    )


def far(d):
    return min(d, 4 - d)


CTX_STEPS = sorted(
    ((y, x, c) for y in range(4) for x in range(4) for c in range(2) if y or x or c),
    key=lambda o: -(3 * far(o[0]) + 3 * far(o[1]) + o[2]),
)
ALL_STEPS = sorted(
    ((y, x, c, z) for y in range(4) for x in range(4) for c in range(2) for z in range(4) if y or x or c or z),
    key=lambda o: -(3 * far(o[0]) + 3 * far(o[1]) + o[2] + 3 * far(o[3])),
)


def iota(shape, axis):
    return lax.broadcasted_iota(jnp.int32, shape, axis)


def kernel(
    src_hbm, ids_hbm, wts_hbm, lens_hbm, we_hbm, wq_hbm, wo_hbm, forget_hbm, cot_hbm,
    out, gqkv, gout, gemb,
    src, ids, wts, lens, we, wq, wo, forget, cot,
    stage_mix, recv_mix, glast, recv_g, m_local, recv_m, stage_s, recv_s,
    rise, fade, decay, m4, mgs, u_ref, a_ref, y_ref, gcol, at, bt, ct, ctbig, gram, kk, wop, y0,
    zall, recv_z, xall, recv_x, zrow, recv_zh, yxrow, recv_yx,
    spare_g, spare_m, spare_s, spare_z, spare_x, spare_yx, spare_zh,
    in_sem, mix_s, mix_r, g_s, g_r, m_s, m_r, s_s, s_r, z_s, z_r, x_s, x_r, zh_s, zh_r, yx_s, yx_r,
):
    ctx = lax.axis_index("ctx")
    mix = lax.axis_index("mix")
    me = ctx * NMIX + mix
    plane = ctx // 8

    moves = [
        (ids_hbm, ids), (wts_hbm, wts), (lens_hbm, lens),
        (we_hbm, we), (wq_hbm, wq), (wo_hbm, wo), (cot_hbm, cot),
    ]
    moves = [(src_hbm.at[:, s], src.at[s]) for s in range(LOCAL_SOURCES)] + moves
    moves += [(forget_hbm.at[b], forget.at[pl.ds(b * HEADS, HEADS)]) for b in range(LB)]
    copies = [pltpu.make_async_copy(a, b, in_sem.at[i]) for i, (a, b) in enumerate(moves)]
    part_loads, weight_loads, cot_load, gate_loads = copies[:7], copies[7:10], copies[10], copies[11:]
    for copy in part_loads + gate_loads + weight_loads + [cot_load]:
        copy.start()

    ys = [lax.rem(ctx // 8 + d, 4) * 8 for d in range(4)]
    xs = [lax.rem(ctx // 2 + d, 4) * 2 for d in range(4)]
    cs = [lax.rem(ctx + d, 2) for d in range(2)]
    zs = [lax.rem(mix + d, NMIX) for d in range(NMIX)]
    ctx_partners = [ys[y] + xs[x] + cs[c] for y, x, c in CTX_STEPS]
    all_partners = [(ys[y] + xs[x] + cs[c], zs[z]) for y, x, c, z in ALL_STEPS]
    plane_partners = [(ys[y] + xs[x] + cs[c], zs[z]) for y, x, c, z in ALL_STEPS if y == 0]

    barrier = pltpu.get_barrier_semaphore()
    for other in ctx_partners:
        pl.semaphore_signal(barrier, inc=1, device_id=(other, mix), device_id_type=MESH)
    for other in zs[1:]:
        pl.semaphore_signal(barrier, inc=1, device_id=(ctx, other), device_id_type=MESH)

    for load in part_loads:
        load.wait()
    place = ctx * STEPS + 4 * iota((64, 128), 0) + iota((64, 128), 1) // PATCH
    for b in range(LB * NMIX):
        part = jnp.zeros((64, 128), F32)
        for j in range(TERMS):
            slot = ids[j, b] - mix * LOCAL_SOURCES
            held = jnp.clip(slot, 0, LOCAL_SOURCES - 1)
            weight = jnp.where(slot == held, wts[j, b], 0.0)
            part = part + jnp.where(place < lens[j, b], weight, 0.0) * src[held]
        stage_mix[b] = part

    pl.semaphore_wait(barrier, NCTX - 1 + NMIX - 1)

    own_mix = pltpu.make_async_copy(stage_mix.at[pl.ds(LB * mix, LB)], recv_mix.at[mix], mix_r)
    own_mix.start()
    for other in (zs[2], zs[1], zs[3]):
        pltpu.make_async_remote_copy(
            stage_mix.at[pl.ds(LB * other, LB)], recv_mix.at[mix], mix_s, mix_r,
            device_id=(ctx, other), device_id_type=MESH,
        ).start()

    def spare_copy(part, spare, send):
        pltpu.make_async_copy(part, spare, send).start()

    def ctx_rows(spare, src_ref, dst_ref, send, recv, src_row, dst_row):
        for other in ctx_partners:
            pltpu.make_async_remote_copy(
                src_ref.at[pl.ds(src_row(other), 2)], dst_ref.at[pl.ds(dst_row, 2)], send, recv,
                device_id=(other, mix), device_id_type=MESH,
            ).start()
        spare_copy(src_ref.at[pl.ds(src_row(ctx), 2)], spare, send)
        pltpu.make_async_copy(
            src_ref.at[pl.ds(src_row(ctx), 2)], dst_ref.at[pl.ds(dst_row, 2)], recv
        ).start()

    for load in gate_loads:
        load.wait()
    growth = jnp.log1p(forget[...] - 1.0)
    lanes = iota((LB * HEADS, STEPS), 1)
    for k in (1, 2, 4, 8, 16, 32, 64, 128):
        growth = growth + jnp.where(lanes >= k, pltpu.roll(growth, k, 1), 0.0)
    for b in range(LB):
        col = jnp.concatenate(
            [
                jnp.broadcast_to(growth[b * HEADS + h : b * HEADS + h + 1], (PATCH, STEPS))
                for h in range(HEADS)
            ],
            axis=0,
        ).T
        gcol[b] = col
        last = col[STEPS - 1 : STEPS]
        glast[b : b + 1] = last
        rise[b] = jnp.exp(col)
        fade[b] = jnp.exp(last - col)

    ctx_rows(spare_g, glast, recv_g, g_s, g_r, lambda other: 0, 2 * ctx)

    for load in weight_loads:
        load.wait()
    wt = mm(we[...], wq[...]).astype(BF)
    lane = iota((1, HEAD), 1)
    block = iota((HEAD, HEAD), 0) // PATCH == iota((HEAD, HEAD), 1) // PATCH
    heads = [lane // PATCH == h for h in range(HEADS)]
    for h in range(HEADS):
        rows = pl.ds(h * PATCH, PATCH)
        at[rows] = wt[:, h * HEAD : (h + 1) * HEAD]
        bt[rows] = wt[:, WIDTH + h * HEAD : WIDTH + (h + 1) * HEAD]
        piece = wt[:, 2 * WIDTH + h * HEAD : 2 * WIDTH + (h + 1) * HEAD]
        ct[rows] = piece
        for k in range(HEADS):
            ctbig[rows, k * HEAD : (k + 1) * HEAD] = piece if k == h else jnp.zeros_like(piece)
    gram[...] = jnp.where(block, mm(at[...], bt[...], NT), 0.0).astype(BF)
    kk[...] = jnp.where(block, mm(ct[...], ct[...], NT), 0.0).astype(BF)
    wop[...] = mm(ctbig[...], wo[...]).astype(BF)
    causal = iota((STEPS, STEPS), 0) >= iota((STEPS, STEPS), 1)
    for b in range(LB):
        for h in range(HEADS):
            diff = gcol[b][:, h * PATCH : h * PATCH + 1] - growth[b * HEADS + h : b * HEADS + h + 1]
            decay[b * HEADS + h] = jnp.where(causal, jnp.exp(diff), 0.0)

    pltpu.make_async_copy(recv_mix, recv_mix, mix_r).wait()
    spread = (lax.rem(iota((HEAD, HEAD), 0), PATCH) == lax.rem(iota((HEAD, HEAD), 1), PATCH)).astype(BF)
    pick = (iota((STEPS, 64), 0) // 4 == iota((STEPS, 64), 1)).astype(BF)
    mine = lax.rem(iota((STEPS, HEAD), 0), 4) == iota((STEPS, HEAD), 1) // PATCH
    for b in range(LB):
        packed = ((recv_mix[0, b] + recv_mix[1, b]) + (recv_mix[2, b] + recv_mix[3, b])).astype(BF)
        lone = jnp.where(mine, mm(pick, packed), 0.0).astype(BF)
        rows = mm(lone, spread)
        m4[pl.ds(b * STEPS, STEPS)] = rows.astype(BF)
        faded = (rows * fade[b]).astype(BF)
        m_local[pl.ds(b * PATCH, PATCH)] = mm(rows.astype(BF), faded, TN)[:PATCH]
    ctx_rows(spare_m, m_local, recv_m, m_s, m_r, lambda other: 2 * other, 2 * ctx)

    def inside(b):
        rows = pl.ds(b * STEPS, STEPS)
        mb = m4[rows]
        mg = mm(mb, gram[...])
        mgs[rows] = (mg * rise[b]).astype(BF)
        mgb = mg.astype(BF)
        total = jnp.zeros((STEPS, HEAD), F32)
        for h in range(HEADS):
            score = mm(jnp.where(heads[h], mgb, jnp.zeros_like(mgb)), mb, NT)
            score = (score * decay[b * HEADS + h]).astype(BF)
            total = total + mm(score, jnp.where(heads[h], mb, jnp.zeros_like(mb)))
        u_ref[rows] = total

    inside(0)
    cot_load.wait()
    y0[...] = mm(cot[...], wop[...], NT)

    pltpu.make_async_copy(recv_g, recv_g, g_r).wait()
    pltpu.make_async_copy(recv_m, recv_m, m_r).wait()
    own_b = ctx // (NCTX // LB)
    state = jnp.zeros((2, HEAD), F32)
    for j in range(NCTX):
        stage_s[2 * j : 2 * j + 2] = state
        state = jnp.exp(recv_g[pl.ds(2 * j + own_b, 1)]) * state + recv_m[2 * j : 2 * j + 2]
    ctx_rows(spare_s, stage_s, recv_s, s_s, s_r, lambda other: 2 * other, 2 * ctx)
    inside(1)
    pltpu.make_async_copy(recv_s, recv_s, s_r).wait()

    memory = []
    for b in range(LB):
        part = recv_s[pl.ds(b * PATCH, PATCH)]
        memory.append(
            jnp.where(block, jnp.concatenate([part] * HEADS, axis=0), 0.0).astype(BF)
        )
        rows = pl.ds(b * STEPS, STEPS)
        u_ref[rows] = u_ref[rows] + mm(mgs[rows], memory[b])
    u = u_ref[...]
    ub = u.astype(BF)
    read = mm(ub, ctbig[...])
    sums = (iota((WIDTH, HEAD), 0) // HEAD == iota((WIDTH, HEAD), 1) // PATCH).astype(BF)
    square = mm((read * read).astype(BF), sums) * (1.0 / HEAD)
    inv = lax.rsqrt(square + EPS)
    n = u * inv
    nb = n.astype(BF)
    dots = mm((y0[...] * u).astype(BF), block.astype(BF)) * (1.0 / HEAD)
    def repeat(square_block):
        kept = jnp.where(block, square_block, 0.0)
        kept = kept + pltpu.roll(kept, 64, 1)
        return kept + pltpu.roll(kept, 32, 1)

    def scatter(source, target, send, recv, partners):
        for other, level in partners:
            pltpu.make_async_remote_copy(
                source.at[pl.ds(other * NMIX + level, 1)], target.at[pl.ds(me, 1)], send, recv,
                device_id=(other, level), device_id_type=MESH,
            ).start()

    zall[:, :WIDTH] = mm(nb, cot[...], TN)
    zall[:, WIDTH:] = repeat(mm((n * (inv * dots)).astype(BF), nb, TN))
    pltpu.make_async_copy(zall.at[pl.ds(me, 1)], recv_z.at[pl.ds(me, 1)], z_r).start()
    spare_copy(zall.at[pl.ds(me, 1)], spare_z, z_s)
    scatter(zall, recv_z, z_s, z_r, all_partners[:7])

    y = inv * (y0[...] - inv * (inv * dots) * mm(ub, kk[...]))
    y_ref[...] = y
    for b in range(LB):
        rows = pl.ds(b * STEPS, STEPS)
        mb = m4[rows]
        yb = y_ref[rows]
        yh = yb.astype(BF)
        total = mm((yb * rise[b]).astype(BF), memory[b])
        for h in range(HEADS):
            share = 7 + 15 * (b * HEADS + h)
            scatter(zall, recv_z, z_s, z_r, all_partners[share : share + 15])
            left = mm(jnp.where(heads[h], yh, jnp.zeros_like(yh)), mb, NT)
            left = (left * decay[b * HEADS + h]).astype(BF)
            total = total + mm(left, jnp.where(heads[h], mb, jnp.zeros_like(mb)))
        a_ref[rows] = total.astype(BF)
    xall[...] = repeat(mm(m4[...], a_ref[...], TN))
    scatter(xall, recv_x, x_s, x_r, all_partners)
    pltpu.make_async_copy(xall.at[pl.ds(me, 1)], recv_x.at[pl.ds(me, 1)], x_r).start()
    spare_copy(xall.at[pl.ds(me, 1)], spare_x, x_s)

    out[...] = mm(nb, wop[...]).astype(BF)

    w_head = wo[pl.ds(plane * HEAD, HEAD)]
    c_head = ct[pl.ds(plane * PATCH, PATCH)]
    chosen = (iota((16, HEAD), 1) == 16 * lax.rem(ctx, 8) + iota((16, HEAD), 0)).astype(BF)
    c_rows = mm(chosen, c_head, NT).astype(BF)
    column = (iota((16, WIDTH), 1) == ctx * 16 + iota((16, WIDTH), 0)).astype(BF)
    embed_rows = mm(column, jnp.concatenate([we[...]] * HEADS, axis=0), NT).astype(BF)
    tall = jnp.concatenate([jnp.where(heads[h], embed_rows, jnp.zeros_like(embed_rows)) for h in range(HEADS)], axis=0)
    qkv_rows = wq[pl.ds(ctx * 16, 16)]
    long = jnp.concatenate(
        [
            jnp.concatenate(
                [qkv_rows[:, j * WIDTH + h * HEAD : j * WIDTH + (h + 1) * HEAD] for j in range(3)], axis=1
            )
            for h in range(HEADS)
        ],
        axis=0,
    )

    pltpu.make_async_copy(recv_z, recv_z, z_r).wait()
    row = jnp.sum(recv_z[...], axis=0, keepdims=True)
    fine = row[:, :WIDTH]
    zrow[...] = fine
    local = lax.rem(me, NCTX)

    for partner in plane_partners:
        pltpu.make_async_remote_copy(
            zrow, recv_zh.at[pl.ds(local, 1)], zh_s, zh_r, device_id=partner, device_id_type=MESH
        ).start()
    spare_copy(zrow, spare_zh, zh_s)
    pltpu.make_async_copy(zrow, recv_zh.at[pl.ds(local, 1)], zh_r).start()

    high = fine.astype(BF)
    low = (fine - high.astype(F32)).astype(BF)
    yxrow[:, :HEAD] = mm(high, w_head, NT) + mm(low, w_head, NT) - mm(row[:, WIDTH : WIDTH + PATCH].astype(BF), c_head)
    pltpu.make_async_copy(recv_x, recv_x, x_r).wait()
    yxrow[:, HEAD:] = jnp.sum(recv_x[...], axis=0, keepdims=True)
    for partner in all_partners:
        pltpu.make_async_remote_copy(
            yxrow, recv_yx.at[pl.ds(me, 1)], yx_s, yx_r, device_id=partner, device_id_type=MESH
        ).start()
    spare_copy(yxrow, spare_yx, yx_s)
    pltpu.make_async_copy(yxrow, recv_yx.at[pl.ds(me, 1)], yx_r).start()
    pltpu.make_async_copy(recv_yx, recv_yx, yx_r).wait()
    x_block = jnp.where(block, recv_yx[:, HEAD:], 0.0).astype(BF)
    yq = mm(x_block, bt[...])
    yk = mm(x_block, at[...], TN)
    ys = jnp.concatenate([yq, yk, recv_yx[:, :HEAD]], axis=1).astype(BF)
    wide = mm(tall, ys)
    for h in range(HEADS):
        for j in range(3):
            gqkv[:, j * WIDTH + h * HEAD : j * WIDTH + (h + 1) * HEAD] = wide[
                16 * h : 16 * h + 16, j * HEAD : (j + 1) * HEAD
            ]
    tops = mm(long, ys, NT)
    folded = jnp.zeros((16, HEAD), F32)
    for h in range(HEADS):
        folded = folded + jnp.where(heads[h], tops[16 * h : 16 * h + 16], 0.0)
    folded = folded + pltpu.roll(folded, 64, 1)
    folded = folded + pltpu.roll(folded, 32, 1)
    gemb[...] = folded[:, :PATCH]
    pltpu.make_async_copy(recv_zh, recv_zh, zh_r).wait()
    gout[...] = mm(c_rows, recv_zh[...].astype(BF))

    sent_mix = stage_mix.at[pl.ds(0, LB * (NMIX - 1))]
    pltpu.make_async_copy(sent_mix, sent_mix, mix_s).wait()
    for ref, sem in (
        (recv_g, g_s), (recv_m, m_s), (recv_s, s_s), (recv_z, z_s), (recv_x, x_s), (recv_yx, yx_s), (recv_zh, zh_s)
    ):
        pltpu.make_async_copy(ref, ref, sem).wait()


def hand_on(*refs):
    copies = [pltpu.make_async_copy(refs[i], refs[4 + i], refs[8].at[i]) for i in range(4)]
    for copy in copies:
        copy.start()
    for copy in copies:
        copy.wait()


def shards(
    sources, source_ids, mix_weights, source_lengths, w_embed, w_qkv, w_out, forget, cotangent
):
    packed = sources.reshape(LOCAL_SOURCES, STEPS * PATCH // 128, 128).transpose(1, 0, 2)
    vm = pltpu.VMEM
    sm = pltpu.SMEM
    dma = pltpu.SemaphoreType.DMA
    results = pl.pallas_call(
        kernel,
        out_shape=tuple(vm(shape, kind) for shape, kind in RESULTS),
        in_specs=[pl.BlockSpec(memory_space=pl.ANY)] * 9,
        out_specs=(pl.BlockSpec(memory_space=pltpu.VMEM),) * 4,
        scratch_shapes=[
            vm((LOCAL_SOURCES, 64, 128), F32),
            sm((TERMS, LB * NMIX), jnp.int32),
            sm((TERMS, LB * NMIX), F32),
            sm((TERMS, LB * NMIX), jnp.int32),
            vm((PATCH, WIDTH), BF),
            vm((WIDTH, 3 * WIDTH), BF),
            vm((WIDTH, WIDTH), BF),
            vm((LB * HEADS, STEPS), F32),
            vm((ROWS, WIDTH), BF),
            vm((LB * NMIX, 64, 128), F32),
            vm((NMIX, LB, 64, 128), F32),
            vm((LB, HEAD), F32),
            vm((2 * NCTX, HEAD), F32),
            vm((2 * NCTX, HEAD), F32),
            vm((2 * NCTX, HEAD), F32),
            vm((2 * NCTX, HEAD), F32),
            vm((2 * NCTX, HEAD), F32),
            vm((LB, STEPS, HEAD), F32),
            vm((LB, STEPS, HEAD), F32),
            vm((LB * HEADS, STEPS, STEPS), F32),
            vm((ROWS, HEAD), BF),
            vm((ROWS, HEAD), BF),
            vm((ROWS, HEAD), F32),
            vm((ROWS, HEAD), BF),
            vm((ROWS, HEAD), F32),
            vm((LB, STEPS, HEAD), F32),
            vm((HEAD, HEAD), BF),
            vm((HEAD, HEAD), BF),
            vm((HEAD, HEAD), BF),
            vm((HEAD, WIDTH), BF),
            vm((HEAD, HEAD), BF),
            vm((HEAD, HEAD), BF),
            vm((HEAD, WIDTH), BF),
            vm((ROWS, HEAD), F32),
            vm((NDEV, VX), F32),
            vm((NDEV, VX), F32),
            vm((NDEV, HEAD), F32),
            vm((NDEV, HEAD), F32),
            vm((1, WIDTH), F32),
            vm((NCTX, WIDTH), F32),
            vm((1, 2 * HEAD), F32),
            vm((NDEV, 2 * HEAD), F32),
            vm((2, HEAD), F32),
            vm((2, HEAD), F32),
            vm((2, HEAD), F32),
            vm((1, VX), F32),
            vm((1, HEAD), F32),
            vm((1, 2 * HEAD), F32),
            vm((1, WIDTH), F32),
            dma((13,)),
        ]
        + [dma(())] * 16,
        compiler_params=pltpu.CompilerParams(collective_id=0, has_side_effects=True, vmem_limit_bytes=60 << 20),
        name="whole_step",
    )(
        packed, source_ids.T, mix_weights.T, source_lengths.T, w_embed.T, w_qkv, w_out, forget,
        cotangent.reshape(ROWS, WIDTH),
    )
    output, grad_qkv, grad_out, grad_embed = pl.pallas_call(
        hand_on,
        out_shape=tuple(jax.ShapeDtypeStruct(shape, kind) for shape, kind in RESULTS),
        in_specs=[pl.BlockSpec(memory_space=pltpu.VMEM)] * 4,
        out_specs=(pl.BlockSpec(memory_space=pl.ANY),) * 4,
        scratch_shapes=[dma((4,))],
        name="hand_on",
    )(*[pltpu.with_memory_space_constraint(result, pltpu.VMEM) for result in results])
    return (output.reshape(LB, STEPS, WIDTH), grad_qkv, grad_out, grad_embed)


def solution(mesh):
    placed = (
        P("mix", "ctx"),
        P(),
        P(),
        P(),
        P(),
        P(),
        P(),
        P("mix", None, "ctx"),
        P("mix", "ctx", None),
    )
    return jax.shard_map(
        shards,
        mesh=mesh,
        in_specs=placed,
        out_specs=(P("mix", "ctx", None), P("ctx", None), P("ctx", None), P("ctx", None)),
        check_vma=False,
    )
```

```python
import jax
import jax.numpy as jnp
from jax import lax
from jax.experimental import pallas as pl
from jax.experimental.pallas import tpu as pltpu
from jax.sharding import PartitionSpec as P

EPS = 1e-06
BF = jnp.bfloat16
F32 = jnp.float32
MESH = pl.DeviceIdType.MESH
NCTX = 32
NMIX = 4
NDEV = 128
ROW = 8
PLANES = 4
LB = 2
HEADS = 4
PATCH = 32
STEPS = 256
ROWS = LB * STEPS
HEAD = 128
WIDTH = 512
LOCAL_SOURCES = 4
TERMS = 3
VX = WIDTH + HEAD
RESULTS = (((ROWS, WIDTH), BF), ((16, 3 * WIDTH), F32), ((16, WIDTH), F32), ((16, PATCH), F32))


def mm(left, right, dims=((1,), (0,))):
    return lax.dot_general(left, right, (dims, ((), ())), preferred_element_type=F32)


NT = ((1,), (1,))
TN = ((0,), (0,))


def mm_exact(left, right, dims):
    return lax.dot_general(
        left, right, (dims, ((), ())), precision=lax.Precision.HIGHEST, preferred_element_type=F32
    )


def far(d):
    return min(d, 4 - d)


CTX_STEPS = sorted(
    ((y, x, c) for y in range(4) for x in range(4) for c in range(2) if y or x or c),
    key=lambda o: -(3 * far(o[0]) + 3 * far(o[1]) + o[2]),
)
ALL_STEPS = sorted(
    ((y, x, c, z) for y in range(4) for x in range(4) for c in range(2) for z in range(4) if y or x or c or z),
    key=lambda o: -(3 * far(o[0]) + 3 * far(o[1]) + o[2] + 3 * far(o[3])),
)


def iota(shape, axis):
    return lax.broadcasted_iota(jnp.int32, shape, axis)


def kernel(
    src_hbm, ids_hbm, wts_hbm, lens_hbm, we_hbm, wq_hbm, wo_hbm, forget_hbm, cot_hbm,
    out, gqkv, gout, gemb,
    src, ids, wts, lens, we, wq, wo, forget, cot,
    stage_mix, recv_mix, glast, recv_g, row_gate, recv_r, m_local, recv_m, stage_s, stage_t, recv_s,
    rise, fade, decay, m4, mgs, mgp, u_ref, a_ref, y_ref, gcol, at, bt, ct, ctbig, gram, kk, wop, y0,
    zall, recv_z, zrow, recv_zh, yxrow, recv_yx,
    spare_g, spare_r, spare_m, spare_s, spare_z, spare_yx, spare_zh,
    in_sem, mix_s, mix_r, g_s, g_r, r_s, r_r, m_s, m_r, s_s, s_r, z_s, z_r, zh_s, zh_r, yx_s, yx_r,
):
    ctx = lax.axis_index("ctx")
    mix = lax.axis_index("mix")
    me = ctx * NMIX + mix
    plane = ctx // 8

    moves = [
        (ids_hbm, ids), (wts_hbm, wts), (lens_hbm, lens),
        (we_hbm, we), (wq_hbm, wq), (wo_hbm, wo), (cot_hbm, cot),
    ]
    moves = [(src_hbm.at[:, s], src.at[s]) for s in range(LOCAL_SOURCES)] + moves
    moves += [(forget_hbm.at[b], forget.at[pl.ds(b * HEADS, HEADS)]) for b in range(LB)]
    copies = [pltpu.make_async_copy(a, b, in_sem.at[i]) for i, (a, b) in enumerate(moves)]
    part_loads, weight_loads, cot_load, gate_loads = copies[:7], copies[7:10], copies[10], copies[11:]
    for copy in part_loads + gate_loads + weight_loads + [cot_load]:
        copy.start()

    ys = [lax.rem(ctx // 8 + d, 4) * 8 for d in range(4)]
    xs = [lax.rem(ctx // 2 + d, 4) * 2 for d in range(4)]
    cs = [lax.rem(ctx + d, 2) for d in range(2)]
    zs = [lax.rem(mix + d, NMIX) for d in range(NMIX)]
    all_partners = [(ys[y] + xs[x] + cs[c], zs[z]) for y, x, c, z in ALL_STEPS]
    plane_partners = [(ys[y] + xs[x] + cs[c], zs[z]) for y, x, c, z in ALL_STEPS if y == 0]

    place_x = lax.rem(ctx, 8)
    row_partners = [(xs[x] + cs[c]) for y, x, c in CTX_STEPS if y == 0]

    barrier = pltpu.get_barrier_semaphore()
    for level in zs[1:]:
        pl.semaphore_signal(barrier, inc=1, device_id=(ctx, level), device_id_type=MESH)
    for other in row_partners:
        pl.semaphore_signal(barrier, inc=1, device_id=(ys[0] + other, mix), device_id_type=MESH)
    for base in ys[1:]:
        pl.semaphore_signal(barrier, inc=1, device_id=(base + place_x, mix), device_id_type=MESH)

    for load in part_loads:
        load.wait()
    place = ctx * STEPS + 4 * iota((64, 128), 0) + iota((64, 128), 1) // PATCH
    for b in range(LB * NMIX):
        part = jnp.zeros((64, 128), F32)
        for j in range(TERMS):
            slot = ids[j, b] - mix * LOCAL_SOURCES
            held = jnp.clip(slot, 0, LOCAL_SOURCES - 1)
            weight = jnp.where(slot == held, wts[j, b], 0.0)
            part = part + jnp.where(place < lens[j, b], weight, 0.0) * src[held]
        stage_mix[b] = part

    pl.semaphore_wait(barrier, NMIX - 1 + ROW - 1 + PLANES - 1)

    own_mix = pltpu.make_async_copy(stage_mix.at[pl.ds(LB * mix, LB)], recv_mix.at[mix], mix_r)
    own_mix.start()
    for other in (zs[2], zs[1], zs[3]):
        pltpu.make_async_remote_copy(
            stage_mix.at[pl.ds(LB * other, LB)], recv_mix.at[mix], mix_s, mix_r,
            device_id=(ctx, other), device_id_type=MESH,
        ).start()

    def spare_copy(part, spare, send):
        pltpu.make_async_copy(part, spare, send).start()

    def push(source, target, send, recv, other, level):
        pltpu.make_async_remote_copy(
            source, target, send, recv, device_id=(other, level), device_id_type=MESH
        ).start()

    for load in gate_loads:
        load.wait()
    growth = jnp.log1p(forget[...] - 1.0)
    lanes = iota((LB * HEADS, STEPS), 1)
    for k in (1, 2, 4, 8, 16, 32, 64, 128):
        growth = growth + jnp.where(lanes >= k, pltpu.roll(growth, k, 1), 0.0)
    for b in range(LB):
        col = jnp.concatenate(
            [
                jnp.broadcast_to(growth[b * HEADS + h : b * HEADS + h + 1], (PATCH, STEPS))
                for h in range(HEADS)
            ],
            axis=0,
        ).T
        gcol[b] = col
        last = col[STEPS - 1 : STEPS]
        glast[b : b + 1] = last
        rise[b] = jnp.exp(col)
        fade[b] = jnp.exp(last - col)

    own_g = recv_g.at[pl.ds(LB * place_x, LB)]
    for other in row_partners:
        push(glast, own_g, g_s, g_r, ys[0] + other, mix)
    pltpu.make_async_copy(glast, own_g, g_r).start()
    spare_copy(glast, spare_g, g_s)

    for load in weight_loads:
        load.wait()
    wt = mm(we[...], wq[...]).astype(BF)
    lane = iota((1, HEAD), 1)
    block = iota((HEAD, HEAD), 0) // PATCH == iota((HEAD, HEAD), 1) // PATCH
    heads = [lane // PATCH == h for h in range(HEADS)]
    for h in range(HEADS):
        rows = pl.ds(h * PATCH, PATCH)
        at[rows] = wt[:, h * HEAD : (h + 1) * HEAD]
        bt[rows] = wt[:, WIDTH + h * HEAD : WIDTH + (h + 1) * HEAD]
        piece = wt[:, 2 * WIDTH + h * HEAD : 2 * WIDTH + (h + 1) * HEAD]
        ct[rows] = piece
        for k in range(HEADS):
            ctbig[rows, k * HEAD : (k + 1) * HEAD] = piece if k == h else jnp.zeros_like(piece)
    gram[...] = jnp.where(block, mm(at[...], bt[...], NT), 0.0).astype(BF)
    kk[...] = jnp.where(block, mm(ct[...], ct[...], NT), 0.0).astype(BF)
    wop[...] = mm(ctbig[...], wo[...]).astype(BF)
    causal = iota((STEPS, STEPS), 0) >= iota((STEPS, STEPS), 1)
    for b in range(LB):
        for h in range(HEADS):
            diff = gcol[b][:, h * PATCH : h * PATCH + 1] - growth[b * HEADS + h : b * HEADS + h + 1]
            decay[b * HEADS + h] = jnp.where(causal, jnp.exp(diff), 0.0)

    pltpu.make_async_copy(recv_g, recv_g, g_r).wait()
    gates = [recv_g[LB * q : LB * q + LB] for q in range(ROW)]
    inner = jnp.zeros((LB, HEAD), F32)
    whole = jnp.zeros((LB, HEAD), F32)
    for q in range(ROW):
        inner = inner + jnp.where(q < place_x, gates[q], 0.0)
        whole = whole + gates[q]
    row_gate[...] = whole
    own_r = recv_r.at[pl.ds(LB * plane, LB)]
    for base in ys[1:]:
        push(row_gate, own_r, r_s, r_r, base + place_x, mix)
    pltpu.make_async_copy(row_gate, own_r, r_r).start()
    spare_copy(row_gate, spare_r, r_s)

    pltpu.make_async_copy(recv_mix, recv_mix, mix_r).wait()
    spread = (lax.rem(iota((HEAD, HEAD), 0), PATCH) == lax.rem(iota((HEAD, HEAD), 1), PATCH)).astype(BF)
    pick = (iota((STEPS, 64), 0) // 4 == iota((STEPS, 64), 1)).astype(BF)
    mine = lax.rem(iota((STEPS, HEAD), 0), 4) == iota((STEPS, HEAD), 1) // PATCH
    for b in range(LB):
        packed = ((recv_mix[0, b] + recv_mix[1, b]) + (recv_mix[2, b] + recv_mix[3, b])).astype(BF)
        lone = jnp.where(mine, mm(pick, packed), 0.0).astype(BF)
        rows = mm(lone, spread)
        m4[pl.ds(b * STEPS, STEPS)] = rows.astype(BF)
        faded = (rows * fade[b]).astype(BF)
        m_local[pl.ds(b * PATCH, PATCH)] = mm(rows.astype(BF), faded, TN)[:PATCH]
    own_m = recv_m.at[place_x]
    for other in row_partners:
        push(m_local.at[pl.ds(8 * other, 8)], own_m, m_s, m_r, ys[0] + other, mix)
    mine_m = m_local.at[pl.ds(8 * place_x, 8)]
    pltpu.make_async_copy(mine_m, own_m, m_r).start()
    spare_copy(mine_m, spare_m, m_s)

    def scores(b):
        rows = pl.ds(b * STEPS, STEPS)
        mg = mm(m4[rows], gram[...])
        mgp[rows] = mg.astype(BF)
        mgs[rows] = (mg * rise[b]).astype(BF)

    def inside(b, some, total):
        rows = pl.ds(b * STEPS, STEPS)
        mb, mgb = m4[rows], mgp[rows]
        for h in some:
            score = mm(jnp.where(heads[h], mgb, jnp.zeros_like(mgb)), mb, NT)
            score = (score * decay[b * HEADS + h]).astype(BF)
            part = mm(score, jnp.where(heads[h], mb, jnp.zeros_like(mb)))
            total = part if total is None else total + part
        u_ref[rows] = total

    scores(0)
    inside(0, (0, 1), None)

    pltpu.make_async_copy(recv_m, recv_m, m_r).wait()
    own_b = place_x // (ROW // LB)
    state = jnp.zeros((8, HEAD), F32)
    for q in range(ROW):
        stage_s[q] = state
        state = jnp.exp(recv_g[pl.ds(LB * q + own_b, 1)]) * state + recv_m[q]
    stage_t[...] = state
    own_s = recv_s.at[plane, place_x]
    for y, x, c in CTX_STEPS:
        other = xs[x] + cs[c]
        push(stage_s.at[other] if y == 0 else stage_t, own_s, s_s, s_r, ys[y] + other, mix)
    pltpu.make_async_copy(stage_s.at[place_x], own_s, s_r).start()
    spare_copy(stage_t, spare_s, s_s)

    inside(0, (2, 3), u_ref[pl.ds(0, STEPS)])
    scores(1)
    inside(1, range(HEADS), None)
    cot_load.wait()
    y0[...] = mm(cot[...], wop[...], NT)
    pltpu.make_async_copy(recv_r, recv_r, r_r).wait()
    factors = []
    reach = inner
    for back in range(PLANES):
        factors.append(reach)
        if back < PLANES - 1:
            reach = reach + recv_r[pl.ds(LB * jnp.maximum(plane - 1 - back, 0), LB)]
    pltpu.make_async_copy(recv_s, recv_s, s_r).wait()

    memory = []
    for b in range(LB):
        part = recv_s[plane, b * 4 : b * 4 + 4].reshape(PATCH, HEAD)
        for back in range(1, PLANES):
            earlier = recv_s[jnp.maximum(plane - back, 0), b * 4 : b * 4 + 4].reshape(PATCH, HEAD)
            weight = jnp.where(plane >= back, jnp.exp(factors[back - 1][b : b + 1]), 0.0)
            part = part + weight * earlier
        memory.append(
            jnp.where(block, jnp.concatenate([part] * HEADS, axis=0), 0.0).astype(BF)
        )
        rows = pl.ds(b * STEPS, STEPS)
        u_ref[rows] = u_ref[rows] + mm(mgs[rows], memory[b])
    u = u_ref[...]
    ub = u.astype(BF)
    read = mm(ub, ctbig[...])
    sums = (iota((WIDTH, HEAD), 0) // HEAD == iota((WIDTH, HEAD), 1) // PATCH).astype(BF)
    square = mm((read * read).astype(BF), sums) * (1.0 / HEAD)
    inv = lax.rsqrt(square + EPS)
    n = u * inv
    nb = n.astype(BF)
    dots = mm((y0[...] * u).astype(BF), block.astype(BF)) * (1.0 / HEAD)
    drift = inv * (inv * dots)
    y = inv * (y0[...] - drift * mm(ub, kk[...]))
    y_ref[...] = y
    for b in range(LB):
        rows = pl.ds(b * STEPS, STEPS)
        mb = m4[rows]
        yb = y_ref[rows]
        yh = yb.astype(BF)
        total = mm((yb * rise[b]).astype(BF), memory[b])
        for h in range(HEADS):
            left = mm(jnp.where(heads[h], yh, jnp.zeros_like(yh)), mb, NT)
            left = (left * decay[b * HEADS + h]).astype(BF)
            total = total + mm(left, jnp.where(heads[h], mb, jnp.zeros_like(mb)))
        a_ref[rows] = total.astype(BF)

    def repeat(square_block):
        kept = jnp.where(block, square_block, 0.0)
        kept = kept + pltpu.roll(kept, 64, 1)
        return kept + pltpu.roll(kept, 32, 1)

    zall[:, :WIDTH] = mm(nb, cot[...], TN)
    v_rows = repeat(mm((n * (inv * dots)).astype(BF), nb, TN))
    x_rows = repeat(mm(m4[...], a_ref[...], TN))
    zall[:, WIDTH:] = jnp.where(lane < 64, v_rows, x_rows)

    for other, level in all_partners:
        pltpu.make_async_remote_copy(
            zall.at[pl.ds(other * NMIX + level, 1)], recv_z.at[pl.ds(me, 1)], z_s, z_r,
            device_id=(other, level), device_id_type=MESH,
        ).start()
    spare_copy(zall.at[pl.ds(me, 1)], spare_z, z_s)
    pltpu.make_async_copy(zall.at[pl.ds(me, 1)], recv_z.at[pl.ds(me, 1)], z_r).start()

    out[...] = mm(nb, wop[...]).astype(BF)

    w_head = wo[pl.ds(plane * HEAD, HEAD)]
    c_head = ct[pl.ds(plane * PATCH, PATCH)]
    chosen = (iota((16, HEAD), 1) == 16 * lax.rem(ctx, 8) + iota((16, HEAD), 0)).astype(BF)
    c_rows = mm(chosen, c_head, NT).astype(BF)
    column = (iota((16, WIDTH), 1) == ctx * 16 + iota((16, WIDTH), 0)).astype(BF)
    embed_rows = mm(column, jnp.concatenate([we[...]] * HEADS, axis=0), NT).astype(BF)
    tall = jnp.concatenate([jnp.where(heads[h], embed_rows, jnp.zeros_like(embed_rows)) for h in range(HEADS)], axis=0)
    qkv_rows = wq[pl.ds(ctx * 16, 16)]
    long = jnp.concatenate(
        [
            jnp.concatenate(
                [qkv_rows[:, j * WIDTH + h * HEAD : j * WIDTH + (h + 1) * HEAD] for j in range(3)], axis=1
            )
            for h in range(HEADS)
        ],
        axis=0,
    )

    pltpu.make_async_copy(recv_z, recv_z, z_r).wait()
    row = jnp.sum(recv_z[...], axis=0, keepdims=True)
    zrow[...] = row[:, :WIDTH]
    mixed = row[:, WIDTH:]
    fine = row[:, :WIDTH]
    high = fine.astype(BF)
    low = (fine - high.astype(F32)).astype(BF)
    yv = mm(high, w_head, NT) + mm(low, w_head, NT) - mm(mixed[:, :PATCH].astype(BF), c_head)
    xs = jnp.where(lane < 64, 0.0, mixed)
    yxrow[:, :HEAD] = yv
    yxrow[:, HEAD:] = xs + pltpu.roll(xs, 64, 1)

    for partner in all_partners:
        pltpu.make_async_remote_copy(
            yxrow, recv_yx.at[pl.ds(me, 1)], yx_s, yx_r, device_id=partner, device_id_type=MESH
        ).start()
    spare_copy(yxrow, spare_yx, yx_s)
    pltpu.make_async_copy(yxrow, recv_yx.at[pl.ds(me, 1)], yx_r).start()
    local = lax.rem(me, NCTX)

    for partner in plane_partners:
        pltpu.make_async_remote_copy(
            zrow, recv_zh.at[pl.ds(local, 1)], zh_s, zh_r, device_id=partner, device_id_type=MESH
        ).start()
    spare_copy(zrow, spare_zh, zh_s)
    pltpu.make_async_copy(zrow, recv_zh.at[pl.ds(local, 1)], zh_r).start()

    pltpu.make_async_copy(recv_yx, recv_yx, yx_r).wait()
    x_block = jnp.where(block, recv_yx[:, HEAD:], 0.0).astype(BF)
    yq = mm(x_block, bt[...])
    yk = mm(x_block, at[...], TN)
    ys = jnp.concatenate([yq, yk, recv_yx[:, :HEAD]], axis=1).astype(BF)
    wide = mm(tall, ys)
    for h in range(HEADS):
        for j in range(3):
            gqkv[:, j * WIDTH + h * HEAD : j * WIDTH + (h + 1) * HEAD] = wide[
                16 * h : 16 * h + 16, j * HEAD : (j + 1) * HEAD
            ]
    tops = mm(long, ys, NT)
    folded = jnp.zeros((16, HEAD), F32)
    for h in range(HEADS):
        folded = folded + jnp.where(heads[h], tops[16 * h : 16 * h + 16], 0.0)
    folded = folded + pltpu.roll(folded, 64, 1)
    folded = folded + pltpu.roll(folded, 32, 1)
    gemb[...] = folded[:, :PATCH]
    pltpu.make_async_copy(recv_zh, recv_zh, zh_r).wait()
    gout[...] = mm(c_rows, recv_zh[...].astype(BF))

    sent_mix = stage_mix.at[pl.ds(0, LB * (NMIX - 1))]
    pltpu.make_async_copy(sent_mix, sent_mix, mix_s).wait()
    for ref, sem in (
        (recv_g, g_s), (recv_r, r_s), (recv_m, m_s), (recv_s, s_s), (recv_z, z_s), (recv_yx, yx_s), (recv_zh, zh_s)
    ):
        pltpu.make_async_copy(ref, ref, sem).wait()


def hand_on(*refs):
    copies = [pltpu.make_async_copy(refs[i], refs[4 + i], refs[8].at[i]) for i in range(4)]
    for copy in copies:
        copy.start()
    for copy in copies:
        copy.wait()


def shards(
    sources, source_ids, mix_weights, source_lengths, w_embed, w_qkv, w_out, forget, cotangent
):
    packed = sources.reshape(LOCAL_SOURCES, STEPS * PATCH // 128, 128).transpose(1, 0, 2)
    vm = pltpu.VMEM
    sm = pltpu.SMEM
    dma = pltpu.SemaphoreType.DMA
    results = pl.pallas_call(
        kernel,
        out_shape=tuple(vm(shape, kind) for shape, kind in RESULTS),
        in_specs=[pl.BlockSpec(memory_space=pl.ANY)] * 9,
        out_specs=(pl.BlockSpec(memory_space=pltpu.VMEM),) * 4,
        scratch_shapes=[
            vm((LOCAL_SOURCES, 64, 128), F32),
            sm((TERMS, LB * NMIX), jnp.int32),
            sm((TERMS, LB * NMIX), F32),
            sm((TERMS, LB * NMIX), jnp.int32),
            vm((PATCH, WIDTH), BF),
            vm((WIDTH, 3 * WIDTH), BF),
            vm((WIDTH, WIDTH), BF),
            vm((LB * HEADS, STEPS), F32),
            vm((ROWS, WIDTH), BF),
            vm((LB * NMIX, 64, 128), F32),
            vm((NMIX, LB, 64, 128), F32),
            vm((LB, HEAD), F32),
            vm((LB * ROW, HEAD), F32),
            vm((LB, HEAD), F32),
            vm((LB * PLANES, HEAD), F32),
            vm((LB * PATCH, HEAD), F32),
            vm((ROW, 8, HEAD), F32),
            vm((ROW, 8, HEAD), F32),
            vm((8, HEAD), F32),
            vm((PLANES, ROW, 8, HEAD), F32),
            vm((LB, STEPS, HEAD), F32),
            vm((LB, STEPS, HEAD), F32),
            vm((LB * HEADS, STEPS, STEPS), F32),
            vm((ROWS, HEAD), BF),
            vm((ROWS, HEAD), BF),
            vm((ROWS, HEAD), BF),
            vm((ROWS, HEAD), F32),
            vm((ROWS, HEAD), BF),
            vm((ROWS, HEAD), F32),
            vm((LB, STEPS, HEAD), F32),
            vm((HEAD, HEAD), BF),
            vm((HEAD, HEAD), BF),
            vm((HEAD, HEAD), BF),
            vm((HEAD, WIDTH), BF),
            vm((HEAD, HEAD), BF),
            vm((HEAD, HEAD), BF),
            vm((HEAD, WIDTH), BF),
            vm((ROWS, HEAD), F32),
            vm((NDEV, VX), F32),
            vm((NDEV, VX), F32),
            vm((1, WIDTH), F32),
            vm((NCTX, WIDTH), F32),
            vm((1, 2 * HEAD), F32),
            vm((NDEV, 2 * HEAD), F32),
            vm((LB, HEAD), F32),
            vm((LB, HEAD), F32),
            vm((8, HEAD), F32),
            vm((8, HEAD), F32),
            vm((1, VX), F32),
            vm((1, 2 * HEAD), F32),
            vm((1, WIDTH), F32),
            dma((13,)),
        ]
        + [dma(())] * 16,
        compiler_params=pltpu.CompilerParams(collective_id=0, has_side_effects=True, vmem_limit_bytes=60 << 20),
        name="whole_step",
    )(
        packed, source_ids.T, mix_weights.T, source_lengths.T, w_embed.T, w_qkv, w_out, forget,
        cotangent.reshape(ROWS, WIDTH),
    )
    output, grad_qkv, grad_out, grad_embed = pl.pallas_call(
        hand_on,
        out_shape=tuple(jax.ShapeDtypeStruct(shape, kind) for shape, kind in RESULTS),
        in_specs=[pl.BlockSpec(memory_space=pltpu.VMEM)] * 4,
        out_specs=(pl.BlockSpec(memory_space=pl.ANY),) * 4,
        scratch_shapes=[dma((4,))],
        name="hand_on",
    )(*[pltpu.with_memory_space_constraint(result, pltpu.VMEM) for result in results])
    return (output.reshape(LB, STEPS, WIDTH), grad_qkv, grad_out, grad_embed)


def solution(mesh):
    placed = (
        P("mix", "ctx"),
        P(),
        P(),
        P(),
        P(),
        P(),
        P(),
        P("mix", None, "ctx"),
        P("mix", "ctx", None),
    )
    return jax.shard_map(
        shards,
        mesh=mesh,
        in_specs=placed,
        out_specs=(P("mix", "ctx", None), P("ctx", None), P("ctx", None), P("ctx", None)),
        check_vma=False,
    )
```

```python
import jax
import jax.numpy as jnp
from jax import lax
from jax.experimental import pallas as pl
from jax.experimental.pallas import tpu as pltpu
from jax.sharding import PartitionSpec as P

EPS = 1e-06
BF = jnp.bfloat16
F32 = jnp.float32
MESH = pl.DeviceIdType.MESH
NCTX = 32
NMIX = 4
NDEV = 128
ROW = 8
PLANES = 4
LB = 2
HEADS = 4
PATCH = 32
STEPS = 256
ROWS = LB * STEPS
HEAD = 128
WIDTH = 512
LOCAL_SOURCES = 4
TERMS = 3
VX = WIDTH + HEAD
RESULTS = (((ROWS, WIDTH), BF), ((16, 3 * WIDTH), F32), ((16, WIDTH), F32), ((16, PATCH), F32))


def mm(left, right, dims=((1,), (0,))):
    return lax.dot_general(left, right, (dims, ((), ())), preferred_element_type=F32)


NT = ((1,), (1,))
TN = ((0,), (0,))


def mm_exact(left, right, dims):
    return lax.dot_general(
        left, right, (dims, ((), ())), precision=lax.Precision.HIGHEST, preferred_element_type=F32
    )


def far(d):
    return min(d, 4 - d)


CTX_STEPS = sorted(
    ((y, x, c) for y in range(4) for x in range(4) for c in range(2) if y or x or c),
    key=lambda o: -(3 * far(o[0]) + 3 * far(o[1]) + o[2]),
)
ALL_STEPS = sorted(
    ((y, x, c, z) for y in range(4) for x in range(4) for c in range(2) for z in range(4) if y or x or c or z),
    key=lambda o: -(3 * far(o[0]) + 3 * far(o[1]) + o[2] + 3 * far(o[3])),
)


def iota(shape, axis):
    return lax.broadcasted_iota(jnp.int32, shape, axis)


def kernel(
    src_hbm, ids_hbm, wts_hbm, lens_hbm, we_hbm, wq_hbm, wo_hbm, forget_hbm, cot_hbm,
    out, gqkv, gout, gemb,
    src, ids, wts, lens, we, wq, wo, forget, cot,
    stage_mix, recv_mix, glast, recv_g, row_gate, recv_r, m_local, recv_m, stage_s, stage_t, recv_s,
    rise, fade, decay, m4, mgs, mgp, u_ref, a_ref, y_ref, gcol, at, bt, ct, ctbig, gram, kk, wop, y0,
    zall, recv_z, zrow, recv_zh, yxrow, recv_yx,
    spare_g, spare_r, spare_m, spare_s, spare_z, spare_yx, spare_zh,
    in_sem, mix_s, mix_r, g_s, g_r, r_s, r_r, m_s, m_r, s_s, s_r, z_s, z_r, zh_s, zh_r, yx_s, yx_r,
):
    ctx = lax.axis_index("ctx")
    mix = lax.axis_index("mix")
    me = ctx * NMIX + mix
    plane = ctx // 8

    moves = [
        (ids_hbm, ids), (wts_hbm, wts), (lens_hbm, lens),
        (we_hbm, we), (wq_hbm, wq), (wo_hbm, wo), (cot_hbm, cot),
    ]
    moves = [(src_hbm.at[:, s], src.at[s]) for s in range(LOCAL_SOURCES)] + moves
    moves += [(forget_hbm.at[b], forget.at[pl.ds(b * HEADS, HEADS)]) for b in range(LB)]
    copies = [pltpu.make_async_copy(a, b, in_sem.at[i]) for i, (a, b) in enumerate(moves)]
    part_loads, weight_loads, cot_load, gate_loads = copies[:7], copies[7:10], copies[10], copies[11:]
    for copy in part_loads + gate_loads + weight_loads + [cot_load]:
        copy.start()

    ys = [lax.rem(ctx // 8 + d, 4) * 8 for d in range(4)]
    xs = [lax.rem(ctx // 2 + d, 4) * 2 for d in range(4)]
    cs = [lax.rem(ctx + d, 2) for d in range(2)]
    zs = [lax.rem(mix + d, NMIX) for d in range(NMIX)]
    all_partners = [(ys[y] + xs[x] + cs[c], zs[z]) for y, x, c, z in ALL_STEPS]
    plane_partners = [(ys[y] + xs[x] + cs[c], zs[z]) for y, x, c, z in ALL_STEPS if y == 0]

    place_x = lax.rem(ctx, 8)
    row_partners = [(xs[x] + cs[c]) for y, x, c in CTX_STEPS if y == 0]

    barrier = pltpu.get_barrier_semaphore()
    for level in zs[1:]:
        pl.semaphore_signal(barrier, inc=1, device_id=(ctx, level), device_id_type=MESH)
    for other in row_partners:
        pl.semaphore_signal(barrier, inc=1, device_id=(ys[0] + other, mix), device_id_type=MESH)
    for base in ys[1:]:
        pl.semaphore_signal(barrier, inc=1, device_id=(base + place_x, mix), device_id_type=MESH)

    for load in part_loads:
        load.wait()
    place = ctx * STEPS + 4 * iota((64, 128), 0) + iota((64, 128), 1) // PATCH
    for b in range(LB * NMIX):
        part = jnp.zeros((64, 128), F32)
        for j in range(TERMS):
            slot = ids[j, b] - mix * LOCAL_SOURCES
            held = jnp.clip(slot, 0, LOCAL_SOURCES - 1)
            weight = jnp.where(slot == held, wts[j, b], 0.0)
            part = part + jnp.where(place < lens[j, b], weight, 0.0) * src[held]
        stage_mix[b] = part

    pl.semaphore_wait(barrier, NMIX - 1 + ROW - 1 + PLANES - 1)

    for b in range(LB):
        landing = recv_mix.at[b, mix]
        for level in (zs[2], zs[1], zs[3]):
            pltpu.make_async_remote_copy(
                stage_mix.at[LB * level + b], landing, mix_s, mix_r.at[b],
                device_id=(ctx, level), device_id_type=MESH,
            ).start()
        pltpu.make_async_copy(stage_mix.at[LB * mix + b], landing, mix_r.at[b]).start()

    def spare_copy(part, spare, send):
        pltpu.make_async_copy(part, spare, send).start()

    def push(source, target, send, recv, other, level):
        pltpu.make_async_remote_copy(
            source, target, send, recv, device_id=(other, level), device_id_type=MESH
        ).start()

    for load in gate_loads:
        load.wait()
    growth = jnp.log1p(forget[...] - 1.0)
    lanes = iota((LB * HEADS, STEPS), 1)
    for k in (1, 2, 4, 8, 16, 32, 64, 128):
        growth = growth + jnp.where(lanes >= k, pltpu.roll(growth, k, 1), 0.0)
    for b in range(LB):
        col = jnp.concatenate(
            [
                jnp.broadcast_to(growth[b * HEADS + h : b * HEADS + h + 1], (PATCH, STEPS))
                for h in range(HEADS)
            ],
            axis=0,
        ).T
        gcol[b] = col
        last = col[STEPS - 1 : STEPS]
        glast[b : b + 1] = last
        rise[b] = jnp.exp(col)
        fade[b] = jnp.exp(last - col)

    own_g = recv_g.at[pl.ds(LB * place_x, LB)]
    for other in row_partners:
        push(glast, own_g, g_s, g_r, ys[0] + other, mix)
    pltpu.make_async_copy(glast, own_g, g_r).start()
    spare_copy(glast, spare_g, g_s)

    for load in weight_loads:
        load.wait()
    wt = mm(we[...], wq[...]).astype(BF)
    lane = iota((1, HEAD), 1)
    block = iota((HEAD, HEAD), 0) // PATCH == iota((HEAD, HEAD), 1) // PATCH
    heads = [lane // PATCH == h for h in range(HEADS)]
    for h in range(HEADS):
        rows = pl.ds(h * PATCH, PATCH)
        at[rows] = wt[:, h * HEAD : (h + 1) * HEAD]
        bt[rows] = wt[:, WIDTH + h * HEAD : WIDTH + (h + 1) * HEAD]
        piece = wt[:, 2 * WIDTH + h * HEAD : 2 * WIDTH + (h + 1) * HEAD]
        ct[rows] = piece
        for k in range(HEADS):
            ctbig[rows, k * HEAD : (k + 1) * HEAD] = piece if k == h else jnp.zeros_like(piece)
    gram[...] = jnp.where(block, mm(at[...], bt[...], NT), 0.0).astype(BF)
    square = jnp.where(block, mm(ct[...], ct[...], NT), 0.0)
    kk[0] = square.astype(BF)
    kk[1] = (square - kk[0].astype(F32)).astype(BF)
    wop[...] = mm(ctbig[...], wo[...]).astype(BF)
    causal = iota((STEPS, STEPS), 0) >= iota((STEPS, STEPS), 1)
    for b in range(LB):
        for h in range(HEADS):
            diff = gcol[b][:, h * PATCH : h * PATCH + 1] - growth[b * HEADS + h : b * HEADS + h + 1]
            decay[b * HEADS + h] = jnp.where(causal, jnp.exp(diff), 0.0)

    pltpu.make_async_copy(recv_g, recv_g, g_r).wait()
    gates = [recv_g[LB * q : LB * q + LB] for q in range(ROW)]
    inner = jnp.zeros((LB, HEAD), F32)
    whole = jnp.zeros((LB, HEAD), F32)
    for q in range(ROW):
        inner = inner + jnp.where(q < place_x, gates[q], 0.0)
        whole = whole + gates[q]
    row_gate[...] = whole
    own_r = recv_r.at[pl.ds(LB * plane, LB)]
    for base in ys[1:]:
        push(row_gate, own_r, r_s, r_r, base + place_x, mix)
    pltpu.make_async_copy(row_gate, own_r, r_r).start()
    spare_copy(row_gate, spare_r, r_s)

    spread = (lax.rem(iota((HEAD, HEAD), 0), PATCH) == lax.rem(iota((HEAD, HEAD), 1), PATCH)).astype(BF)
    pick = (iota((STEPS, 64), 0) // 4 == iota((STEPS, 64), 1)).astype(BF)
    mine = lax.rem(iota((STEPS, HEAD), 0), 4) == iota((STEPS, HEAD), 1) // PATCH
    for b in range(LB):
        pltpu.make_async_copy(recv_mix.at[b], recv_mix.at[b], mix_r.at[b]).wait()
        packed = ((recv_mix[b, 0] + recv_mix[b, 1]) + (recv_mix[b, 2] + recv_mix[b, 3])).astype(BF)
        lone = jnp.where(mine, mm(pick, packed), 0.0).astype(BF)
        rows = mm(lone, spread)
        m4[pl.ds(b * STEPS, STEPS)] = rows.astype(BF)
        faded = (rows * fade[b]).astype(BF)
        m_local[pl.ds(b * PATCH, PATCH)] = mm(rows.astype(BF), faded, TN)[:PATCH]
    own_m = recv_m.at[place_x]
    for other in row_partners:
        push(m_local.at[pl.ds(8 * other, 8)], own_m, m_s, m_r, ys[0] + other, mix)
    mine_m = m_local.at[pl.ds(8 * place_x, 8)]
    pltpu.make_async_copy(mine_m, own_m, m_r).start()
    spare_copy(mine_m, spare_m, m_s)

    def scores(b):
        rows = pl.ds(b * STEPS, STEPS)
        mg = mm(m4[rows], gram[...])
        mgp[rows] = mg.astype(BF)
        mgs[rows] = (mg * rise[b]).astype(BF)

    def inside(b, some, total):
        rows = pl.ds(b * STEPS, STEPS)
        mb, mgb = m4[rows], mgp[rows]
        for h in some:
            score = mm(jnp.where(heads[h], mgb, jnp.zeros_like(mgb)), mb, NT)
            score = (score * decay[b * HEADS + h]).astype(BF)
            part = mm(score, jnp.where(heads[h], mb, jnp.zeros_like(mb)))
            total = part if total is None else total + part
        u_ref[rows] = total

    scores(0)
    inside(0, (0, 1), None)

    pltpu.make_async_copy(recv_m, recv_m, m_r).wait()
    own_b = place_x // (ROW // LB)
    state = jnp.zeros((8, HEAD), F32)
    for q in range(ROW):
        stage_s[q] = state
        state = jnp.exp(recv_g[pl.ds(LB * q + own_b, 1)]) * state + recv_m[q]
    stage_t[...] = state
    own_s = recv_s.at[plane, place_x]
    for y, x, c in CTX_STEPS:
        other = xs[x] + cs[c]
        push(stage_s.at[other] if y == 0 else stage_t, own_s, s_s, s_r, ys[y] + other, mix)
    pltpu.make_async_copy(stage_s.at[place_x], own_s, s_r).start()
    spare_copy(stage_t, spare_s, s_s)

    inside(0, (2, 3), u_ref[pl.ds(0, STEPS)])
    scores(1)
    inside(1, range(HEADS), None)
    cot_load.wait()
    y0[...] = mm(cot[...], wop[...], NT)
    pltpu.make_async_copy(recv_r, recv_r, r_r).wait()
    factors = []
    reach = inner
    for back in range(PLANES):
        factors.append(reach)
        if back < PLANES - 1:
            reach = reach + recv_r[pl.ds(LB * jnp.maximum(plane - 1 - back, 0), LB)]
    pltpu.make_async_copy(recv_s, recv_s, s_r).wait()

    memory = []
    for b in range(LB):
        part = recv_s[plane, b * 4 : b * 4 + 4].reshape(PATCH, HEAD)
        for back in range(1, PLANES):
            earlier = recv_s[jnp.maximum(plane - back, 0), b * 4 : b * 4 + 4].reshape(PATCH, HEAD)
            weight = jnp.where(plane >= back, jnp.exp(factors[back - 1][b : b + 1]), 0.0)
            part = part + weight * earlier
        memory.append(
            jnp.where(block, jnp.concatenate([part] * HEADS, axis=0), 0.0).astype(BF)
        )
        rows = pl.ds(b * STEPS, STEPS)
        u_ref[rows] = u_ref[rows] + mm(mgs[rows], memory[b])
    u = u_ref[...]
    ub = u.astype(BF)
    ku = mm(ub, kk[0]) + mm(ub, kk[1])
    ones = block.astype(BF)
    square = ub.astype(F32) * ku
    high = square.astype(BF)
    low = (square - high.astype(F32)).astype(BF)
    square = (mm(high, ones) + mm(low, ones)) * (1.0 / HEAD)
    inv = lax.rsqrt(jnp.maximum(square, 0.0) + EPS)
    n = u * inv
    nb = n.astype(BF)
    dots = mm((y0[...] * u).astype(BF), ones) * (1.0 / HEAD)
    drift = inv * (inv * dots)
    y = inv * (y0[...] - drift * ku)
    y_ref[...] = y
    for b in range(LB):
        rows = pl.ds(b * STEPS, STEPS)
        mb = m4[rows]
        yb = y_ref[rows]
        yh = yb.astype(BF)
        total = mm((yb * rise[b]).astype(BF), memory[b])
        for h in range(HEADS):
            left = mm(jnp.where(heads[h], yh, jnp.zeros_like(yh)), mb, NT)
            left = (left * decay[b * HEADS + h]).astype(BF)
            total = total + mm(left, jnp.where(heads[h], mb, jnp.zeros_like(mb)))
        a_ref[rows] = total.astype(BF)

    def repeat(square_block):
        kept = jnp.where(block, square_block, 0.0)
        kept = kept + pltpu.roll(kept, 64, 1)
        return kept + pltpu.roll(kept, 32, 1)

    zall[:, :WIDTH] = mm(nb, cot[...], TN)
    v_rows = repeat(mm((n * (inv * dots)).astype(BF), nb, TN))
    x_rows = repeat(mm(m4[...], a_ref[...], TN))
    zall[:, WIDTH:] = jnp.where(lane < 64, v_rows, x_rows)

    for other, level in all_partners:
        pltpu.make_async_remote_copy(
            zall.at[pl.ds(other * NMIX + level, 1)], recv_z.at[pl.ds(me, 1)], z_s, z_r,
            device_id=(other, level), device_id_type=MESH,
        ).start()
    spare_copy(zall.at[pl.ds(me, 1)], spare_z, z_s)
    pltpu.make_async_copy(zall.at[pl.ds(me, 1)], recv_z.at[pl.ds(me, 1)], z_r).start()

    out[...] = mm(nb, wop[...]).astype(BF)

    w_head = wo[pl.ds(plane * HEAD, HEAD)]
    c_head = ct[pl.ds(plane * PATCH, PATCH)]
    chosen = (iota((16, HEAD), 1) == 16 * lax.rem(ctx, 8) + iota((16, HEAD), 0)).astype(BF)
    c_rows = mm(chosen, c_head, NT).astype(BF)
    column = (iota((16, WIDTH), 1) == ctx * 16 + iota((16, WIDTH), 0)).astype(BF)
    embed_rows = mm(column, jnp.concatenate([we[...]] * HEADS, axis=0), NT).astype(BF)
    tall = jnp.concatenate([jnp.where(heads[h], embed_rows, jnp.zeros_like(embed_rows)) for h in range(HEADS)], axis=0)
    qkv_rows = wq[pl.ds(ctx * 16, 16)]
    long = jnp.concatenate(
        [
            jnp.concatenate(
                [qkv_rows[:, j * WIDTH + h * HEAD : j * WIDTH + (h + 1) * HEAD] for j in range(3)], axis=1
            )
            for h in range(HEADS)
        ],
        axis=0,
    )

    pltpu.make_async_copy(recv_z, recv_z, z_r).wait()
    row = jnp.sum(recv_z[...], axis=0, keepdims=True)
    zrow[...] = row[:, :WIDTH]
    mixed = row[:, WIDTH:]
    fine = row[:, :WIDTH]
    high = fine.astype(BF)
    low = (fine - high.astype(F32)).astype(BF)
    yv = mm(high, w_head, NT) + mm(low, w_head, NT) - mm(mixed[:, :PATCH].astype(BF), c_head)
    xs = jnp.where(lane < 64, 0.0, mixed)
    yxrow[:, :HEAD] = yv
    yxrow[:, HEAD:] = xs + pltpu.roll(xs, 64, 1)

    for partner in all_partners:
        pltpu.make_async_remote_copy(
            yxrow, recv_yx.at[pl.ds(me, 1)], yx_s, yx_r, device_id=partner, device_id_type=MESH
        ).start()
    spare_copy(yxrow, spare_yx, yx_s)
    pltpu.make_async_copy(yxrow, recv_yx.at[pl.ds(me, 1)], yx_r).start()
    local = lax.rem(me, NCTX)

    for partner in plane_partners:
        pltpu.make_async_remote_copy(
            zrow, recv_zh.at[pl.ds(local, 1)], zh_s, zh_r, device_id=partner, device_id_type=MESH
        ).start()
    spare_copy(zrow, spare_zh, zh_s)
    pltpu.make_async_copy(zrow, recv_zh.at[pl.ds(local, 1)], zh_r).start()

    pltpu.make_async_copy(recv_zh, recv_zh, zh_r).wait()
    gout[...] = mm(c_rows, recv_zh[...].astype(BF))
    pltpu.make_async_copy(recv_yx, recv_yx, yx_r).wait()
    x_block = jnp.where(block, recv_yx[:, HEAD:], 0.0).astype(BF)
    yq = mm(x_block, bt[...])
    yk = mm(x_block, at[...], TN)
    ys = jnp.concatenate([yq, yk, recv_yx[:, :HEAD]], axis=1).astype(BF)
    wide = mm(tall, ys)
    for h in range(HEADS):
        for j in range(3):
            gqkv[:, j * WIDTH + h * HEAD : j * WIDTH + (h + 1) * HEAD] = wide[
                16 * h : 16 * h + 16, j * HEAD : (j + 1) * HEAD
            ]
    tops = mm(long, ys, NT)
    folded = jnp.zeros((16, HEAD), F32)
    for h in range(HEADS):
        folded = folded + jnp.where(heads[h], tops[16 * h : 16 * h + 16], 0.0)
    folded = folded + pltpu.roll(folded, 64, 1)
    folded = folded + pltpu.roll(folded, 32, 1)
    gemb[...] = folded[:, :PATCH]

    sent_mix = stage_mix.at[pl.ds(0, LB * (NMIX - 1))]
    pltpu.make_async_copy(sent_mix, sent_mix, mix_s).wait()
    for ref, sem in (
        (recv_g, g_s), (recv_r, r_s), (recv_m, m_s), (recv_s, s_s), (recv_z, z_s), (recv_yx, yx_s), (recv_zh, zh_s)
    ):
        pltpu.make_async_copy(ref, ref, sem).wait()


def hand_on(*refs):
    moves = [(refs[i], refs[4 + i]) for i in range(1, 4)]
    for i in range(4):
        rows = pl.ds(i * ROWS // 4, ROWS // 4)
        moves.append((refs[0].at[rows], refs[4].at[rows]))
    copies = [pltpu.make_async_copy(a, b, refs[8].at[i]) for i, (a, b) in enumerate(moves)]
    for copy in copies:
        copy.start()
    for copy in copies:
        copy.wait()


def shards(
    sources, source_ids, mix_weights, source_lengths, w_embed, w_qkv, w_out, forget, cotangent
):
    packed = sources.reshape(LOCAL_SOURCES, STEPS * PATCH // 128, 128).transpose(1, 0, 2)
    vm = pltpu.VMEM
    sm = pltpu.SMEM
    dma = pltpu.SemaphoreType.DMA
    results = pl.pallas_call(
        kernel,
        out_shape=tuple(vm(shape, kind) for shape, kind in RESULTS),
        in_specs=[pl.BlockSpec(memory_space=pl.ANY)] * 9,
        out_specs=(pl.BlockSpec(memory_space=pltpu.VMEM),) * 4,
        scratch_shapes=[
            vm((LOCAL_SOURCES, 64, 128), F32),
            sm((TERMS, LB * NMIX), jnp.int32),
            sm((TERMS, LB * NMIX), F32),
            sm((TERMS, LB * NMIX), jnp.int32),
            vm((PATCH, WIDTH), BF),
            vm((WIDTH, 3 * WIDTH), BF),
            vm((WIDTH, WIDTH), BF),
            vm((LB * HEADS, STEPS), F32),
            vm((ROWS, WIDTH), BF),
            vm((LB * NMIX, 64, 128), F32),
            vm((LB, NMIX, 64, 128), F32),
            vm((LB, HEAD), F32),
            vm((LB * ROW, HEAD), F32),
            vm((LB, HEAD), F32),
            vm((LB * PLANES, HEAD), F32),
            vm((LB * PATCH, HEAD), F32),
            vm((ROW, 8, HEAD), F32),
            vm((ROW, 8, HEAD), F32),
            vm((8, HEAD), F32),
            vm((PLANES, ROW, 8, HEAD), F32),
            vm((LB, STEPS, HEAD), F32),
            vm((LB, STEPS, HEAD), F32),
            vm((LB * HEADS, STEPS, STEPS), F32),
            vm((ROWS, HEAD), BF),
            vm((ROWS, HEAD), BF),
            vm((ROWS, HEAD), BF),
            vm((ROWS, HEAD), F32),
            vm((ROWS, HEAD), BF),
            vm((ROWS, HEAD), F32),
            vm((LB, STEPS, HEAD), F32),
            vm((HEAD, HEAD), BF),
            vm((HEAD, HEAD), BF),
            vm((HEAD, HEAD), BF),
            vm((HEAD, WIDTH), BF),
            vm((HEAD, HEAD), BF),
            vm((2, HEAD, HEAD), BF),
            vm((HEAD, WIDTH), BF),
            vm((ROWS, HEAD), F32),
            vm((NDEV, VX), F32),
            vm((NDEV, VX), F32),
            vm((1, WIDTH), F32),
            vm((NCTX, WIDTH), F32),
            vm((1, 2 * HEAD), F32),
            vm((NDEV, 2 * HEAD), F32),
            vm((LB, HEAD), F32),
            vm((LB, HEAD), F32),
            vm((8, HEAD), F32),
            vm((8, HEAD), F32),
            vm((1, VX), F32),
            vm((1, 2 * HEAD), F32),
            vm((1, WIDTH), F32),
            dma((13,)),
        ]
        + [dma(()), dma((LB,))]
        + [dma(())] * 14,
        compiler_params=pltpu.CompilerParams(collective_id=0, has_side_effects=True, vmem_limit_bytes=60 << 20),
        name="whole_step",
    )(
        packed, source_ids.T, mix_weights.T, source_lengths.T, w_embed.T, w_qkv, w_out, forget,
        cotangent.reshape(ROWS, WIDTH),
    )
    output, grad_qkv, grad_out, grad_embed = pl.pallas_call(
        hand_on,
        out_shape=tuple(jax.ShapeDtypeStruct(shape, kind) for shape, kind in RESULTS),
        in_specs=[pl.BlockSpec(memory_space=pltpu.VMEM)] * 4,
        out_specs=(pl.BlockSpec(memory_space=pl.ANY),) * 4,
        scratch_shapes=[dma((7,))],
        name="hand_on",
    )(*[pltpu.with_memory_space_constraint(result, pltpu.VMEM) for result in results])
    return (output.reshape(LB, STEPS, WIDTH), grad_qkv, grad_out, grad_embed)


def solution(mesh):
    placed = (
        P("mix", "ctx"),
        P(),
        P(),
        P(),
        P(),
        P(),
        P(),
        P("mix", None, "ctx"),
        P("mix", "ctx", None),
    )
    return jax.shard_map(
        shards,
        mesh=mesh,
        in_specs=placed,
        out_specs=(P("mix", "ctx", None), P("ctx", None), P("ctx", None), P("ctx", None)),
        check_vma=False,
    )
```

```python
import jax
import jax.numpy as jnp
from jax import lax
from jax.experimental import pallas as pl
from jax.experimental.pallas import tpu as pltpu
from jax.sharding import PartitionSpec as P

EPS = 1e-06
BF = jnp.bfloat16
F32 = jnp.float32
MESH = pl.DeviceIdType.MESH
NCTX = 32
NMIX = 4
NDEV = 128
ROW = 8
PLANES = 4
LB = 2
HEADS = 4
PATCH = 32
STEPS = 256
ROWS = LB * STEPS
HEAD = 128
WIDTH = 512
LOCAL_SOURCES = 4
TERMS = 3
RESULTS = (((ROWS, WIDTH), BF), ((16, 3 * WIDTH), F32), ((16, WIDTH), F32), ((16, PATCH), F32))


def mm(left, right, dims=((1,), (0,))):
    return lax.dot_general(left, right, (dims, ((), ())), preferred_element_type=F32)


NT = ((1,), (1,))
TN = ((0,), (0,))


def mm_exact(left, right, dims):
    return lax.dot_general(
        left, right, (dims, ((), ())), precision=lax.Precision.HIGHEST, preferred_element_type=F32
    )


def far(d):
    return min(d, 4 - d)


CTX_STEPS = sorted(
    ((y, x, c) for y in range(4) for x in range(4) for c in range(2) if y or x or c),
    key=lambda o: -(3 * far(o[0]) + 3 * far(o[1]) + o[2]),
)
ALL_STEPS = sorted(
    ((y, x, c, z) for y in range(4) for x in range(4) for c in range(2) for z in range(4) if y or x or c or z),
    key=lambda o: -(3 * far(o[0]) + 3 * far(o[1]) + o[2] + 3 * far(o[3])),
)


def iota(shape, axis):
    return lax.broadcasted_iota(jnp.int32, shape, axis)


def kernel(
    src_hbm, ids_hbm, wts_hbm, lens_hbm, we_hbm, wq_hbm, wo_hbm, forget_hbm, cot_hbm,
    out, gqkv, gout, gemb,
    src, ids, wts, lens, we, wq, wo, forget, cot,
    stage_mix, recv_mix, glast, recv_g, row_gate, recv_r, m_local, recv_m, stage_s, stage_t, recv_s,
    rise, fade, decay, m4, mgs, mgp, u_ref, a_ref, y_ref, gcol, at, bt, ct, ctbig, gram, kk, wop, y0,
    zmat, zpeer, zsum, recv_z, vxall, recv_x, zrow, recv_zh, yxrow, recv_yx,
    spare_g, spare_r, spare_m, spare_s, spare_z, spare_x, spare_yx, spare_zh,
    in_sem, mix_s, mix_r, g_s, g_r, r_s, r_r, m_s, m_r, s_s, s_r, zc_s, zc_r, z_s, z_r, x_s, x_r, zh_s, zh_r, yx_s, yx_r,
):
    ctx = lax.axis_index("ctx")
    mix = lax.axis_index("mix")
    me = ctx * NMIX + mix
    plane = ctx // 8

    moves = [
        (ids_hbm, ids), (wts_hbm, wts), (lens_hbm, lens),
        (we_hbm, we), (wq_hbm, wq), (wo_hbm, wo), (cot_hbm, cot),
    ]
    moves = [(src_hbm.at[:, s], src.at[s]) for s in range(LOCAL_SOURCES)] + moves
    moves += [(forget_hbm.at[b], forget.at[pl.ds(b * HEADS, HEADS)]) for b in range(LB)]
    copies = [pltpu.make_async_copy(a, b, in_sem.at[i]) for i, (a, b) in enumerate(moves)]
    part_loads, weight_loads, cot_load, gate_loads = copies[:7], copies[7:10], copies[10], copies[11:]
    for copy in part_loads + gate_loads + weight_loads + [cot_load]:
        copy.start()

    ys = [lax.rem(ctx // 8 + d, 4) * 8 for d in range(4)]
    xs = [lax.rem(ctx // 2 + d, 4) * 2 for d in range(4)]
    cs = [lax.rem(ctx + d, 2) for d in range(2)]
    zs = [lax.rem(mix + d, NMIX) for d in range(NMIX)]
    all_partners = [(ys[y] + xs[x] + cs[c], zs[z]) for y, x, c, z in ALL_STEPS]
    plane_partners = [(ys[y] + xs[x] + cs[c], zs[z]) for y, x, c, z in ALL_STEPS if y == 0]

    place_x = lax.rem(ctx, 8)
    all_rows = [(ys[y] * 4 + cs[c] * 16 + xs[x] * 2 + zs[z]) for y, x, c, z in ALL_STEPS]
    own_row = ys[0] * 4 + cs[0] * 16 + xs[0] * 2 + zs[0]
    chip_rows = [ys[y] * 2 + xs[x] * 2 + zs[z] for y, x, c, z in ALL_STEPS]
    own_chip_row = ys[0] * 2 + xs[0] * 2 + zs[0]
    row_partners = [(xs[x] + cs[c]) for y, x, c in CTX_STEPS if y == 0]

    barrier = pltpu.get_barrier_semaphore()
    for level in zs[1:]:
        pl.semaphore_signal(barrier, inc=1, device_id=(ctx, level), device_id_type=MESH)
    for other in row_partners:
        pl.semaphore_signal(barrier, inc=1, device_id=(ys[0] + other, mix), device_id_type=MESH)
    for base in ys[1:]:
        pl.semaphore_signal(barrier, inc=1, device_id=(base + place_x, mix), device_id_type=MESH)

    for load in part_loads:
        load.wait()
    place = ctx * STEPS + 4 * iota((64, 128), 0) + iota((64, 128), 1) // PATCH
    for b in range(LB * NMIX):
        part = jnp.zeros((64, 128), F32)
        for j in range(TERMS):
            slot = ids[j, b] - mix * LOCAL_SOURCES
            held = jnp.clip(slot, 0, LOCAL_SOURCES - 1)
            weight = jnp.where(slot == held, wts[j, b], 0.0)
            part = part + jnp.where(place < lens[j, b], weight, 0.0) * src[held]
        stage_mix[b] = part

    pl.semaphore_wait(barrier, NMIX - 1 + ROW - 1 + PLANES - 1)

    for b in range(LB):
        landing = recv_mix.at[b, mix]
        for level in (zs[2], zs[1], zs[3]):
            pltpu.make_async_remote_copy(
                stage_mix.at[LB * level + b], landing, mix_s, mix_r.at[b],
                device_id=(ctx, level), device_id_type=MESH,
            ).start()
        pltpu.make_async_copy(stage_mix.at[LB * mix + b], landing, mix_r.at[b]).start()

    def spare_copy(part, spare, send):
        pltpu.make_async_copy(part, spare, send).start()

    def push(source, target, send, recv, other, level):
        pltpu.make_async_remote_copy(
            source, target, send, recv, device_id=(other, level), device_id_type=MESH
        ).start()

    for load in gate_loads:
        load.wait()
    growth = jnp.log1p(forget[...] - 1.0)
    lanes = iota((LB * HEADS, STEPS), 1)
    for k in (1, 2, 4, 8, 16, 32, 64, 128):
        growth = growth + jnp.where(lanes >= k, pltpu.roll(growth, k, 1), 0.0)
    for b in range(LB):
        col = jnp.concatenate(
            [
                jnp.broadcast_to(growth[b * HEADS + h : b * HEADS + h + 1], (PATCH, STEPS))
                for h in range(HEADS)
            ],
            axis=0,
        ).T
        gcol[b] = col
        last = col[STEPS - 1 : STEPS]
        glast[b : b + 1] = last
        rise[b] = jnp.exp(col)
        fade[b] = jnp.exp(last - col)

    own_g = recv_g.at[pl.ds(LB * place_x, LB)]
    for other in row_partners:
        push(glast, own_g, g_s, g_r, ys[0] + other, mix)
    pltpu.make_async_copy(glast, own_g, g_r).start()
    spare_copy(glast, spare_g, g_s)

    for load in weight_loads:
        load.wait()
    wt = mm(we[...], wq[...]).astype(BF)
    lane = iota((1, HEAD), 1)
    block = iota((HEAD, HEAD), 0) // PATCH == iota((HEAD, HEAD), 1) // PATCH
    heads = [lane // PATCH == h for h in range(HEADS)]
    for h in range(HEADS):
        rows = pl.ds(h * PATCH, PATCH)
        at[rows] = wt[:, h * HEAD : (h + 1) * HEAD]
        bt[rows] = wt[:, WIDTH + h * HEAD : WIDTH + (h + 1) * HEAD]
        piece = wt[:, 2 * WIDTH + h * HEAD : 2 * WIDTH + (h + 1) * HEAD]
        ct[rows] = piece
        for k in range(HEADS):
            ctbig[rows, k * HEAD : (k + 1) * HEAD] = piece if k == h else jnp.zeros_like(piece)
    gram[...] = jnp.where(block, mm(at[...], bt[...], NT), 0.0).astype(BF)
    square = jnp.where(block, mm(ct[...], ct[...], NT), 0.0)
    kk[0] = square.astype(BF)
    kk[1] = (square - kk[0].astype(F32)).astype(BF)
    wop[...] = mm(ctbig[...], wo[...]).astype(BF)
    causal = iota((STEPS, STEPS), 0) >= iota((STEPS, STEPS), 1)
    for b in range(LB):
        for h in range(HEADS):
            diff = gcol[b][:, h * PATCH : h * PATCH + 1] - growth[b * HEADS + h : b * HEADS + h + 1]
            decay[b * HEADS + h] = jnp.where(causal, jnp.exp(diff), 0.0)

    pltpu.make_async_copy(recv_g, recv_g, g_r).wait()
    gates = [recv_g[LB * q : LB * q + LB] for q in range(ROW)]
    inner = jnp.zeros((LB, HEAD), F32)
    whole = jnp.zeros((LB, HEAD), F32)
    for q in range(ROW):
        inner = inner + jnp.where(q < place_x, gates[q], 0.0)
        whole = whole + gates[q]
    row_gate[...] = whole
    own_r = recv_r.at[pl.ds(LB * plane, LB)]
    for base in ys[1:]:
        push(row_gate, own_r, r_s, r_r, base + place_x, mix)
    pltpu.make_async_copy(row_gate, own_r, r_r).start()
    spare_copy(row_gate, spare_r, r_s)

    spread = (lax.rem(iota((HEAD, HEAD), 0), PATCH) == lax.rem(iota((HEAD, HEAD), 1), PATCH)).astype(BF)
    pick = (iota((STEPS, 64), 0) // 4 == iota((STEPS, 64), 1)).astype(BF)
    mine = lax.rem(iota((STEPS, HEAD), 0), 4) == iota((STEPS, HEAD), 1) // PATCH
    for b in range(LB):
        pltpu.make_async_copy(recv_mix.at[b], recv_mix.at[b], mix_r.at[b]).wait()
        packed = ((recv_mix[b, 0] + recv_mix[b, 1]) + (recv_mix[b, 2] + recv_mix[b, 3])).astype(BF)
        lone = jnp.where(mine, mm(pick, packed), 0.0).astype(BF)
        rows = mm(lone, spread)
        m4[pl.ds(b * STEPS, STEPS)] = rows.astype(BF)
        faded = (rows * fade[b]).astype(BF)
        m_local[pl.ds(b * PATCH, PATCH)] = mm(rows.astype(BF), faded, TN)[:PATCH]
    own_m = recv_m.at[place_x]
    for other in row_partners:
        push(m_local.at[pl.ds(8 * other, 8)], own_m, m_s, m_r, ys[0] + other, mix)
    mine_m = m_local.at[pl.ds(8 * place_x, 8)]
    pltpu.make_async_copy(mine_m, own_m, m_r).start()
    spare_copy(mine_m, spare_m, m_s)

    def scores(b):
        rows = pl.ds(b * STEPS, STEPS)
        mg = mm(m4[rows], gram[...])
        mgp[rows] = mg.astype(BF)
        mgs[rows] = (mg * rise[b]).astype(BF)

    def inside(b, some, total):
        rows = pl.ds(b * STEPS, STEPS)
        mb, mgb = m4[rows], mgp[rows]
        for h in some:
            score = mm(jnp.where(heads[h], mgb, jnp.zeros_like(mgb)), mb, NT)
            score = (score * decay[b * HEADS + h]).astype(BF)
            part = mm(score, jnp.where(heads[h], mb, jnp.zeros_like(mb)))
            total = part if total is None else total + part
        u_ref[rows] = total

    scores(0)
    inside(0, (0, 1), None)

    pltpu.make_async_copy(recv_m, recv_m, m_r).wait()
    own_b = place_x // (ROW // LB)
    state = jnp.zeros((8, HEAD), F32)
    for q in range(ROW):
        stage_s[q] = state
        state = jnp.exp(recv_g[pl.ds(LB * q + own_b, 1)]) * state + recv_m[q]
    stage_t[...] = state
    own_s = recv_s.at[plane, place_x]
    for y, x, c in CTX_STEPS:
        other = xs[x] + cs[c]
        push(stage_s.at[other] if y == 0 else stage_t, own_s, s_s, s_r, ys[y] + other, mix)
    pltpu.make_async_copy(stage_s.at[place_x], own_s, s_r).start()
    spare_copy(stage_t, spare_s, s_s)

    inside(0, (2, 3), u_ref[pl.ds(0, STEPS)])
    scores(1)
    inside(1, range(HEADS), None)
    cot_load.wait()
    y0[...] = mm(cot[...], wop[...], NT)
    pltpu.make_async_copy(recv_r, recv_r, r_r).wait()
    factors = []
    reach = inner
    for back in range(PLANES):
        factors.append(reach)
        if back < PLANES - 1:
            reach = reach + recv_r[pl.ds(LB * jnp.maximum(plane - 1 - back, 0), LB)]
    pltpu.make_async_copy(recv_s, recv_s, s_r).wait()

    memory = []
    for b in range(LB):
        part = recv_s[plane, b * 4 : b * 4 + 4].reshape(PATCH, HEAD)
        for back in range(1, PLANES):
            earlier = recv_s[jnp.maximum(plane - back, 0), b * 4 : b * 4 + 4].reshape(PATCH, HEAD)
            weight = jnp.where(plane >= back, jnp.exp(factors[back - 1][b : b + 1]), 0.0)
            part = part + weight * earlier
        memory.append(
            jnp.where(block, jnp.concatenate([part] * HEADS, axis=0), 0.0).astype(BF)
        )
        rows = pl.ds(b * STEPS, STEPS)
        u_ref[rows] = u_ref[rows] + mm(mgs[rows], memory[b])
    u = u_ref[...]
    ub = u.astype(BF)
    ku = mm(ub, kk[0]) + mm(ub, kk[1])
    ones = block.astype(BF)
    square = ub.astype(F32) * ku
    high = square.astype(BF)
    low = (square - high.astype(F32)).astype(BF)
    square = (mm(high, ones) + mm(low, ones)) * (1.0 / HEAD)
    inv = lax.rsqrt(jnp.maximum(square, 0.0) + EPS)
    n = u * inv
    nb = n.astype(BF)
    dots = mm((y0[...] * u).astype(BF), ones) * (1.0 / HEAD)
    zmat[...] = mm(nb, cot[...], TN).reshape(HEADS, 2, 16, WIDTH)
    push(zmat.at[:, cs[1]], zpeer, zc_s, zc_r, ys[0] + xs[0] + cs[1], mix)

    drift = inv * (inv * dots)
    y = inv * (y0[...] - drift * ku)
    y_ref[...] = y
    for b in range(LB):
        rows = pl.ds(b * STEPS, STEPS)
        mb = m4[rows]
        yb = y_ref[rows]
        yh = yb.astype(BF)
        total = mm((yb * rise[b]).astype(BF), memory[b])
        for h in range(HEADS):
            left = mm(jnp.where(heads[h], yh, jnp.zeros_like(yh)), mb, NT)
            left = (left * decay[b * HEADS + h]).astype(BF)
            total = total + mm(left, jnp.where(heads[h], mb, jnp.zeros_like(mb)))
        a_ref[rows] = total.astype(BF)

    def repeat(square_block):
        kept = jnp.where(block, square_block, 0.0)
        kept = kept + pltpu.roll(kept, 64, 1)
        return kept + pltpu.roll(kept, 32, 1)

    v_rows = repeat(mm((n * (inv * dots)).astype(BF), nb, TN))
    x_rows = repeat(mm(m4[...], a_ref[...], TN))
    vxall[...] = jnp.where(lane < 64, v_rows, x_rows)
    pltpu.make_async_copy(zpeer, zpeer, zc_r).wait()
    zsum[...] = (zmat[:, cs[0]] + zpeer[...]).reshape(NDEV // 2, WIDTH)
    own_z = recv_z.at[pl.ds(own_chip_row, 1)]
    own_x = recv_x.at[pl.ds(own_row, 1)]
    for step, row, chip_row, partner in zip(ALL_STEPS, all_rows, chip_rows, all_partners):
        if step[2] == 0:
            push(zsum.at[pl.ds(chip_row, 1)], own_z, z_s, z_r, *partner)
        push(vxall.at[pl.ds(row, 1)], own_x, x_s, x_r, *partner)
    spare_copy(zsum.at[pl.ds(own_chip_row, 1)], spare_z, z_s)
    spare_copy(vxall.at[pl.ds(own_row, 1)], spare_x, x_s)
    pltpu.make_async_copy(zsum.at[pl.ds(own_chip_row, 1)], own_z, z_r).start()
    pltpu.make_async_copy(vxall.at[pl.ds(own_row, 1)], own_x, x_r).start()

    out[...] = mm(nb, wop[...]).astype(BF)

    w_head = wo[pl.ds(plane * HEAD, HEAD)]
    c_head = ct[pl.ds(plane * PATCH, PATCH)]
    chosen = (iota((16, HEAD), 1) == 16 * lax.rem(ctx, 8) + iota((16, HEAD), 0)).astype(BF)
    c_rows = mm(chosen, c_head, NT).astype(BF)
    column = (iota((16, WIDTH), 1) == ctx * 16 + iota((16, WIDTH), 0)).astype(BF)
    embed_rows = mm(column, jnp.concatenate([we[...]] * HEADS, axis=0), NT).astype(BF)
    tall = jnp.concatenate([jnp.where(heads[h], embed_rows, jnp.zeros_like(embed_rows)) for h in range(HEADS)], axis=0)
    qkv_rows = wq[pl.ds(ctx * 16, 16)]
    long = jnp.concatenate(
        [
            jnp.concatenate(
                [qkv_rows[:, j * WIDTH + h * HEAD : j * WIDTH + (h + 1) * HEAD] for j in range(3)], axis=1
            )
            for h in range(HEADS)
        ],
        axis=0,
    )

    pltpu.make_async_copy(recv_z, recv_z, z_r).wait()
    fine = jnp.sum(recv_z[...], axis=0, keepdims=True)
    zrow[...] = fine
    high = fine.astype(BF)
    low = (fine - high.astype(F32)).astype(BF)
    yv = mm(high, w_head, NT) + mm(low, w_head, NT)
    pltpu.make_async_copy(recv_x, recv_x, x_r).wait()
    mixed = jnp.sum(recv_x[...], axis=0, keepdims=True)
    xs_sum = jnp.where(lane < 64, 0.0, mixed)
    yxrow[:, :HEAD] = yv - mm(mixed[:, :PATCH].astype(BF), c_head)
    yxrow[:, HEAD:] = xs_sum + pltpu.roll(xs_sum, 64, 1)
    own_yx = recv_yx.at[pl.ds(own_row, 1)]
    own_zh = recv_zh.at[pl.ds(lax.rem(own_row, NCTX), 1)]
    for partner in all_partners:
        push(yxrow, own_yx, yx_s, yx_r, *partner)
    for partner in plane_partners:
        push(zrow, own_zh, zh_s, zh_r, *partner)
    spare_copy(yxrow, spare_yx, yx_s)
    spare_copy(zrow, spare_zh, zh_s)
    pltpu.make_async_copy(yxrow, own_yx, yx_r).start()
    pltpu.make_async_copy(zrow, own_zh, zh_r).start()

    pltpu.make_async_copy(recv_zh, recv_zh, zh_r).wait()
    gout[...] = mm(c_rows, recv_zh[...].astype(BF))
    pltpu.make_async_copy(recv_yx, recv_yx, yx_r).wait()
    x_block = jnp.where(block, recv_yx[:, HEAD:], 0.0).astype(BF)
    yq = mm(x_block, bt[...])
    yk = mm(x_block, at[...], TN)
    ys = jnp.concatenate([yq, yk, recv_yx[:, :HEAD]], axis=1).astype(BF)
    wide = mm(tall, ys)
    for h in range(HEADS):
        for j in range(3):
            gqkv[:, j * WIDTH + h * HEAD : j * WIDTH + (h + 1) * HEAD] = wide[
                16 * h : 16 * h + 16, j * HEAD : (j + 1) * HEAD
            ]
    tops = mm(long, ys, NT)
    folded = jnp.zeros((16, HEAD), F32)
    for h in range(HEADS):
        folded = folded + jnp.where(heads[h], tops[16 * h : 16 * h + 16], 0.0)
    folded = folded + pltpu.roll(folded, 64, 1)
    folded = folded + pltpu.roll(folded, 32, 1)
    gemb[...] = folded[:, :PATCH]

    sent_mix = stage_mix.at[pl.ds(0, LB * (NMIX - 1))]
    pltpu.make_async_copy(sent_mix, sent_mix, mix_s).wait()
    for ref, sem in (
        (recv_g, g_s), (recv_r, r_s), (recv_m, m_s), (recv_s, s_s), (zpeer, zc_s), (recv_z, z_s), (recv_x, x_s), (recv_yx, yx_s), (recv_zh, zh_s)
    ):
        pltpu.make_async_copy(ref, ref, sem).wait()


def hand_on(*refs):
    copies = [pltpu.make_async_copy(refs[i], refs[4 + i], refs[8].at[i]) for i in range(4)]
    for copy in copies:
        copy.start()
    for copy in copies:
        copy.wait()


def shards(
    sources, source_ids, mix_weights, source_lengths, w_embed, w_qkv, w_out, forget, cotangent
):
    packed = sources.reshape(LOCAL_SOURCES, STEPS * PATCH // 128, 128).transpose(1, 0, 2)
    vm = pltpu.VMEM
    sm = pltpu.SMEM
    dma = pltpu.SemaphoreType.DMA
    results = pl.pallas_call(
        kernel,
        out_shape=tuple(vm(shape, kind) for shape, kind in RESULTS),
        in_specs=[pl.BlockSpec(memory_space=pl.ANY)] * 9,
        out_specs=(pl.BlockSpec(memory_space=pltpu.VMEM),) * 4,
        scratch_shapes=[
            vm((LOCAL_SOURCES, 64, 128), F32),
            sm((TERMS, LB * NMIX), jnp.int32),
            sm((TERMS, LB * NMIX), F32),
            sm((TERMS, LB * NMIX), jnp.int32),
            vm((PATCH, WIDTH), BF),
            vm((WIDTH, 3 * WIDTH), BF),
            vm((WIDTH, WIDTH), BF),
            vm((LB * HEADS, STEPS), F32),
            vm((ROWS, WIDTH), BF),
            vm((LB * NMIX, 64, 128), F32),
            vm((LB, NMIX, 64, 128), F32),
            vm((LB, HEAD), F32),
            vm((LB * ROW, HEAD), F32),
            vm((LB, HEAD), F32),
            vm((LB * PLANES, HEAD), F32),
            vm((LB * PATCH, HEAD), F32),
            vm((ROW, 8, HEAD), F32),
            vm((ROW, 8, HEAD), F32),
            vm((8, HEAD), F32),
            vm((PLANES, ROW, 8, HEAD), F32),
            vm((LB, STEPS, HEAD), F32),
            vm((LB, STEPS, HEAD), F32),
            vm((LB * HEADS, STEPS, STEPS), F32),
            vm((ROWS, HEAD), BF),
            vm((ROWS, HEAD), BF),
            vm((ROWS, HEAD), BF),
            vm((ROWS, HEAD), F32),
            vm((ROWS, HEAD), BF),
            vm((ROWS, HEAD), F32),
            vm((LB, STEPS, HEAD), F32),
            vm((HEAD, HEAD), BF),
            vm((HEAD, HEAD), BF),
            vm((HEAD, HEAD), BF),
            vm((HEAD, WIDTH), BF),
            vm((HEAD, HEAD), BF),
            vm((2, HEAD, HEAD), BF),
            vm((HEAD, WIDTH), BF),
            vm((ROWS, HEAD), F32),
            vm((HEADS, 2, 16, WIDTH), F32),
            vm((HEADS, 16, WIDTH), F32),
            vm((NDEV // 2, WIDTH), F32),
            vm((NDEV // 2, WIDTH), F32),
            vm((NDEV, HEAD), F32),
            vm((NDEV, HEAD), F32),
            vm((1, WIDTH), F32),
            vm((NCTX, WIDTH), F32),
            vm((1, 2 * HEAD), F32),
            vm((NDEV, 2 * HEAD), F32),
            vm((LB, HEAD), F32),
            vm((LB, HEAD), F32),
            vm((8, HEAD), F32),
            vm((8, HEAD), F32),
            vm((1, WIDTH), F32),
            vm((1, HEAD), F32),
            vm((1, 2 * HEAD), F32),
            vm((1, WIDTH), F32),
            dma((13,)),
        ]
        + [dma(()), dma((LB,))]
        + [dma(())] * 18,
        compiler_params=pltpu.CompilerParams(collective_id=0, has_side_effects=True, vmem_limit_bytes=60 << 20),
        name="whole_step",
    )(
        packed, source_ids.T, mix_weights.T, source_lengths.T, w_embed.T, w_qkv, w_out, forget,
        cotangent.reshape(ROWS, WIDTH),
    )
    output, grad_qkv, grad_out, grad_embed = pl.pallas_call(
        hand_on,
        out_shape=tuple(jax.ShapeDtypeStruct(shape, kind) for shape, kind in RESULTS),
        in_specs=[pl.BlockSpec(memory_space=pltpu.VMEM)] * 4,
        out_specs=(pl.BlockSpec(memory_space=pl.ANY),) * 4,
        scratch_shapes=[dma((4,))],
        name="hand_on",
    )(*[pltpu.with_memory_space_constraint(result, pltpu.VMEM) for result in results])
    return (output.reshape(LB, STEPS, WIDTH), grad_qkv, grad_out, grad_embed)


def solution(mesh):
    placed = (
        P("mix", "ctx"),
        P(),
        P(),
        P(),
        P(),
        P(),
        P(),
        P("mix", None, "ctx"),
        P("mix", "ctx", None),
    )
    return jax.shard_map(
        shards,
        mesh=mesh,
        in_specs=placed,
        out_specs=(P("mix", "ctx", None), P("ctx", None), P("ctx", None), P("ctx", None)),
        check_vma=False,
    )
```

```python
import jax
import jax.numpy as jnp
from jax import lax
from jax.experimental import pallas as pl
from jax.experimental.pallas import tpu as pltpu
from jax.sharding import PartitionSpec as P

EPS = 1e-06
BF = jnp.bfloat16
F32 = jnp.float32
MESH = pl.DeviceIdType.MESH
NCTX = 32
NMIX = 4
NDEV = 128
ROW = 8
PLANES = 4
LB = 2
HEADS = 4
PATCH = 32
STEPS = 256
ROWS = LB * STEPS
HEAD = 128
WIDTH = 512
LOCAL_SOURCES = 4
TERMS = 3
RESULTS = (((ROWS, WIDTH), BF), ((16, 3 * WIDTH), F32), ((16, WIDTH), F32), ((16, PATCH), F32))


def mm(left, right, dims=((1,), (0,))):
    return lax.dot_general(left, right, (dims, ((), ())), preferred_element_type=F32)


NT = ((1,), (1,))
TN = ((0,), (0,))


def mm_exact(left, right, dims):
    return lax.dot_general(
        left, right, (dims, ((), ())), precision=lax.Precision.HIGHEST, preferred_element_type=F32
    )


def far(d):
    return min(d, 4 - d)


CTX_STEPS = sorted(
    ((y, x, c) for y in range(4) for x in range(4) for c in range(2) if y or x or c),
    key=lambda o: -(3 * far(o[0]) + 3 * far(o[1]) + o[2]),
)
ALL_STEPS = sorted(
    ((y, x, c, z) for y in range(4) for x in range(4) for c in range(2) for z in range(4) if y or x or c or z),
    key=lambda o: -(3 * far(o[0]) + 3 * far(o[1]) + o[2] + 3 * far(o[3])),
)


def iota(shape, axis):
    return lax.broadcasted_iota(jnp.int32, shape, axis)


def kernel(
    src_hbm, ids_hbm, wts_hbm, lens_hbm, we_hbm, wq_hbm, wo_hbm, forget_hbm, cot_hbm,
    out, gqkv, gout, gemb,
    src, ids, wts, lens, we, wq, wo, forget, cot,
    stage_mix, recv_mix, glast, recv_g, row_gate, recv_r, m_local, recv_m, stage_s, stage_t, recv_s,
    rise, fade, decay, m4, mgs, mgp, u_ref, mt, y_ref, gcol, at, bt, ct, ctbig, gram, kk, wop, y0,
    zmat, zpeer, zsum, recv_z, vxall, recv_x, zrow, recv_zh, yxrow, recv_yx,
    spare_g, spare_r, spare_m, spare_s, spare_z, spare_x, spare_yx, spare_zh,
    in_sem, mix_s, mix_r, g_s, g_r, r_s, r_r, m_s, m_r, s_s, s_r, zc_s, zc_r, z_s, z_r, x_s, x_r, zh_s, zh_r, yx_s, yx_r,
):
    ctx = lax.axis_index("ctx")
    mix = lax.axis_index("mix")
    me = ctx * NMIX + mix
    plane = ctx // 8

    moves = [
        (ids_hbm, ids), (wts_hbm, wts), (lens_hbm, lens),
        (we_hbm, we), (wq_hbm, wq), (wo_hbm, wo), (cot_hbm, cot),
    ]
    moves = [(src_hbm.at[:, s], src.at[s]) for s in range(LOCAL_SOURCES)] + moves
    moves += [(forget_hbm.at[b], forget.at[pl.ds(b * HEADS, HEADS)]) for b in range(LB)]
    copies = [pltpu.make_async_copy(a, b, in_sem.at[i]) for i, (a, b) in enumerate(moves)]
    part_loads, weight_loads, cot_load, gate_loads = copies[:7], copies[7:10], copies[10], copies[11:]
    for copy in part_loads + gate_loads + weight_loads + [cot_load]:
        copy.start()

    ys = [lax.rem(ctx // 8 + d, 4) * 8 for d in range(4)]
    xs = [lax.rem(ctx // 2 + d, 4) * 2 for d in range(4)]
    cs = [lax.rem(ctx + d, 2) for d in range(2)]
    zs = [lax.rem(mix + d, NMIX) for d in range(NMIX)]
    all_partners = [(ys[y] + xs[x] + cs[c], zs[z]) for y, x, c, z in ALL_STEPS]
    plane_partners = [(ys[y] + xs[x] + cs[c], zs[z]) for y, x, c, z in ALL_STEPS if y == 0]

    place_x = lax.rem(ctx, 8)
    all_rows = [(ys[y] * 4 + cs[c] * 16 + xs[x] * 2 + zs[z]) for y, x, c, z in ALL_STEPS]
    own_row = ys[0] * 4 + cs[0] * 16 + xs[0] * 2 + zs[0]
    chip_rows = [ys[y] * 2 + xs[x] * 2 + zs[z] for y, x, c, z in ALL_STEPS]
    own_chip_row = ys[0] * 2 + xs[0] * 2 + zs[0]
    row_partners = [(xs[x] + cs[c]) for y, x, c in CTX_STEPS if y == 0]

    barrier = pltpu.get_barrier_semaphore()
    for level in zs[1:]:
        pl.semaphore_signal(barrier, inc=1, device_id=(ctx, level), device_id_type=MESH)
    for other in row_partners:
        pl.semaphore_signal(barrier, inc=1, device_id=(ys[0] + other, mix), device_id_type=MESH)
    for base in ys[1:]:
        pl.semaphore_signal(barrier, inc=1, device_id=(base + place_x, mix), device_id_type=MESH)

    for load in part_loads:
        load.wait()
    place = ctx * STEPS + 4 * iota((64, 128), 0) + iota((64, 128), 1) // PATCH
    for b in range(LB * NMIX):
        part = jnp.zeros((64, 128), F32)
        for j in range(TERMS):
            slot = ids[j, b] - mix * LOCAL_SOURCES
            held = jnp.clip(slot, 0, LOCAL_SOURCES - 1)
            weight = jnp.where(slot == held, wts[j, b], 0.0)
            part = part + jnp.where(place < lens[j, b], weight, 0.0) * src[held]
        stage_mix[b] = part

    pl.semaphore_wait(barrier, NMIX - 1 + ROW - 1 + PLANES - 1)

    for b in range(LB):
        landing = recv_mix.at[b, mix]
        for level in (zs[2], zs[1], zs[3]):
            pltpu.make_async_remote_copy(
                stage_mix.at[LB * level + b], landing, mix_s, mix_r.at[b],
                device_id=(ctx, level), device_id_type=MESH,
            ).start()
        pltpu.make_async_copy(stage_mix.at[LB * mix + b], landing, mix_r.at[b]).start()

    def spare_copy(part, spare, send):
        pltpu.make_async_copy(part, spare, send).start()

    def push(source, target, send, recv, other, level):
        pltpu.make_async_remote_copy(
            source, target, send, recv, device_id=(other, level), device_id_type=MESH
        ).start()

    for load in gate_loads:
        load.wait()
    growth = jnp.log1p(forget[...] - 1.0)
    lanes = iota((LB * HEADS, STEPS), 1)
    for k in (1, 2, 4, 8, 16, 32, 64, 128):
        growth = growth + jnp.where(lanes >= k, pltpu.roll(growth, k, 1), 0.0)
    for b in range(LB):
        col = jnp.concatenate(
            [
                jnp.broadcast_to(growth[b * HEADS + h : b * HEADS + h + 1], (PATCH, STEPS))
                for h in range(HEADS)
            ],
            axis=0,
        ).T
        gcol[b] = col
        last = col[STEPS - 1 : STEPS]
        glast[b : b + 1] = last
        rise[b] = jnp.exp(col)
        fade[b] = jnp.exp(last - col)

    own_g = recv_g.at[pl.ds(LB * place_x, LB)]
    for other in row_partners:
        push(glast, own_g, g_s, g_r, ys[0] + other, mix)
    pltpu.make_async_copy(glast, own_g, g_r).start()
    spare_copy(glast, spare_g, g_s)

    for load in weight_loads:
        load.wait()
    wt = mm(we[...], wq[...]).astype(BF)
    lane = iota((1, HEAD), 1)
    block = iota((HEAD, HEAD), 0) // PATCH == iota((HEAD, HEAD), 1) // PATCH
    heads = [lane // PATCH == h for h in range(HEADS)]
    for h in range(HEADS):
        rows = pl.ds(h * PATCH, PATCH)
        at[rows] = wt[:, h * HEAD : (h + 1) * HEAD]
        bt[rows] = wt[:, WIDTH + h * HEAD : WIDTH + (h + 1) * HEAD]
        piece = wt[:, 2 * WIDTH + h * HEAD : 2 * WIDTH + (h + 1) * HEAD]
        ct[rows] = piece
        for k in range(HEADS):
            ctbig[rows, k * HEAD : (k + 1) * HEAD] = piece if k == h else jnp.zeros_like(piece)
    gram[...] = jnp.where(block, mm(at[...], bt[...], NT), 0.0).astype(BF)
    square = jnp.where(block, mm(ct[...], ct[...], NT), 0.0)
    kk[0] = square.astype(BF)
    kk[1] = (square - kk[0].astype(F32)).astype(BF)
    wop[...] = mm(ctbig[...], wo[...]).astype(BF)
    causal = iota((STEPS, STEPS), 0) >= iota((STEPS, STEPS), 1)
    for b in range(LB):
        for h in range(HEADS):
            diff = gcol[b][:, h * PATCH : h * PATCH + 1] - growth[b * HEADS + h : b * HEADS + h + 1]
            decay[b * HEADS + h] = jnp.where(causal, jnp.exp(diff), 0.0)

    pltpu.make_async_copy(recv_g, recv_g, g_r).wait()
    gates = [recv_g[LB * q : LB * q + LB] for q in range(ROW)]
    inner = jnp.zeros((LB, HEAD), F32)
    whole = jnp.zeros((LB, HEAD), F32)
    for q in range(ROW):
        inner = inner + jnp.where(q < place_x, gates[q], 0.0)
        whole = whole + gates[q]
    row_gate[...] = whole
    own_r = recv_r.at[pl.ds(LB * plane, LB)]
    for base in ys[1:]:
        push(row_gate, own_r, r_s, r_r, base + place_x, mix)
    pltpu.make_async_copy(row_gate, own_r, r_r).start()
    spare_copy(row_gate, spare_r, r_s)

    spread = (lax.rem(iota((HEAD, HEAD), 0), PATCH) == lax.rem(iota((HEAD, HEAD), 1), PATCH)).astype(BF)
    pick = (iota((STEPS, 64), 0) // 4 == iota((STEPS, 64), 1)).astype(BF)
    mine = lax.rem(iota((STEPS, HEAD), 0), 4) == iota((STEPS, HEAD), 1) // PATCH
    for b in range(LB):
        pltpu.make_async_copy(recv_mix.at[b], recv_mix.at[b], mix_r.at[b]).wait()
        packed = ((recv_mix[b, 0] + recv_mix[b, 1]) + (recv_mix[b, 2] + recv_mix[b, 3])).astype(BF)
        lone = jnp.where(mine, mm(pick, packed), 0.0).astype(BF)
        rows = mm(lone, spread)
        m4[pl.ds(b * STEPS, STEPS)] = rows.astype(BF)
        faded = (rows * fade[b]).astype(BF)
        m_local[pl.ds(b * PATCH, PATCH)] = mm(rows.astype(BF), faded, TN)[:PATCH]
    own_m = recv_m.at[place_x]
    for other in row_partners:
        push(m_local.at[pl.ds(8 * other, 8)], own_m, m_s, m_r, ys[0] + other, mix)
    mine_m = m_local.at[pl.ds(8 * place_x, 8)]
    pltpu.make_async_copy(mine_m, own_m, m_r).start()
    spare_copy(mine_m, spare_m, m_s)

    def scores(b):
        rows = pl.ds(b * STEPS, STEPS)
        mg = mm(m4[rows], gram[...])
        mgp[rows] = mg.astype(BF)
        mgs[rows] = (mg * rise[b]).astype(BF)

    def inside(b, some, total):
        rows = pl.ds(b * STEPS, STEPS)
        mb, mgb = m4[rows], mgp[rows]
        for h in some:
            score = mm(jnp.where(heads[h], mgb, jnp.zeros_like(mgb)), mb, NT)
            score = (score * decay[b * HEADS + h]).astype(BF)
            part = mm(score, jnp.where(heads[h], mb, jnp.zeros_like(mb)))
            total = part if total is None else total + part
        u_ref[rows] = total

    scores(0)
    inside(0, (0, 1), None)

    pltpu.make_async_copy(recv_m, recv_m, m_r).wait()
    own_b = place_x // (ROW // LB)
    state = jnp.zeros((8, HEAD), F32)
    for q in range(ROW):
        stage_s[q] = state
        state = jnp.exp(recv_g[pl.ds(LB * q + own_b, 1)]) * state + recv_m[q]
    stage_t[...] = state
    own_s = recv_s.at[plane, place_x]
    for y, x, c in CTX_STEPS:
        other = xs[x] + cs[c]
        push(stage_s.at[other] if y == 0 else stage_t, own_s, s_s, s_r, ys[y] + other, mix)
    pltpu.make_async_copy(stage_s.at[place_x], own_s, s_r).start()
    spare_copy(stage_t, spare_s, s_s)

    inside(0, (2, 3), u_ref[pl.ds(0, STEPS)])
    scores(1)
    inside(1, range(HEADS), None)
    for b in range(LB):
        mt[b] = m4[pl.ds(b * STEPS, STEPS)].astype(F32).T[:PATCH].astype(BF)
    cot_load.wait()
    y0[...] = mm(cot[...], wop[...], NT)
    pltpu.make_async_copy(recv_r, recv_r, r_r).wait()
    factors = []
    reach = inner
    for back in range(PLANES):
        factors.append(reach)
        if back < PLANES - 1:
            reach = reach + recv_r[pl.ds(LB * jnp.maximum(plane - 1 - back, 0), LB)]
    pltpu.make_async_copy(recv_s, recv_s, s_r).wait()

    memory = []
    for b in range(LB):
        part = recv_s[plane, b * 4 : b * 4 + 4].reshape(PATCH, HEAD)
        for back in range(1, PLANES):
            earlier = recv_s[jnp.maximum(plane - back, 0), b * 4 : b * 4 + 4].reshape(PATCH, HEAD)
            weight = jnp.where(plane >= back, jnp.exp(factors[back - 1][b : b + 1]), 0.0)
            part = part + weight * earlier
        memory.append(
            jnp.where(block, jnp.concatenate([part] * HEADS, axis=0), 0.0).astype(BF)
        )
        rows = pl.ds(b * STEPS, STEPS)
        u_ref[rows] = u_ref[rows] + mm(mgs[rows], memory[b])
    u = u_ref[...]
    ub = u.astype(BF)
    ku = mm(ub, kk[0]) + mm(ub, kk[1])
    ones = block.astype(BF)
    square = ub.astype(F32) * ku
    high = square.astype(BF)
    low = (square - high.astype(F32)).astype(BF)
    square = (mm(high, ones) + mm(low, ones)) * (1.0 / HEAD)
    inv = lax.rsqrt(jnp.maximum(square, 0.0) + EPS)
    n = u * inv
    nb = n.astype(BF)
    dots = mm((y0[...] * u).astype(BF), ones) * (1.0 / HEAD)
    zmat[...] = mm(nb, cot[...], TN).reshape(HEADS, 2, 16, WIDTH)
    push(zmat.at[:, cs[1]], zpeer, zc_s, zc_r, ys[0] + xs[0] + cs[1], mix)

    drift = inv * (inv * dots)
    y = inv * (y0[...] - drift * ku)
    y_ref[...] = y
    inside_x = jnp.zeros((HEAD, HEAD), F32)
    before_x = jnp.zeros((HEAD, HEAD), F32)
    for b in range(LB):
        rows = pl.ds(b * STEPS, STEPS)
        mb = m4[rows]
        yb = y_ref[rows]
        yh = yb.astype(BF)
        stacked = jnp.concatenate([jnp.where(heads[h], yh, jnp.zeros_like(yh)) for h in range(HEADS)], axis=0)
        left = mm(stacked, mb, NT)
        parts = []
        for h in range(HEADS):
            one = (left[h * STEPS : (h + 1) * STEPS] * decay[b * HEADS + h]).astype(BF)
            parts.append(mm(mt[b], one).astype(BF))
        inside_x = inside_x + mm(jnp.concatenate(parts, axis=0), mb)
        risen = mm(mt[b], (yb * rise[b]).astype(BF))
        risen = jnp.where(block, jnp.concatenate([risen] * HEADS, axis=0), 0.0).astype(BF)
        before_x = before_x + mm(risen, memory[b])

    def repeat(square_block):
        kept = jnp.where(block, square_block, 0.0)
        kept = kept + pltpu.roll(kept, 64, 1)
        return kept + pltpu.roll(kept, 32, 1)

    v_rows = repeat(mm((n * (inv * dots)).astype(BF), nb, TN))
    x_rows = inside_x + repeat(before_x)
    vxall[...] = jnp.where(lane < 64, v_rows, x_rows)
    pltpu.make_async_copy(zpeer, zpeer, zc_r).wait()
    zsum[...] = (zmat[:, cs[0]] + zpeer[...]).reshape(NDEV // 2, WIDTH)
    own_z = recv_z.at[pl.ds(own_chip_row, 1)]
    own_x = recv_x.at[pl.ds(own_row, 1)]
    for step, row, chip_row, partner in zip(ALL_STEPS, all_rows, chip_rows, all_partners):
        if step[2] == 0:
            push(zsum.at[pl.ds(chip_row, 1)], own_z, z_s, z_r, *partner)
        push(vxall.at[pl.ds(row, 1)], own_x, x_s, x_r, *partner)
    spare_copy(zsum.at[pl.ds(own_chip_row, 1)], spare_z, z_s)
    spare_copy(vxall.at[pl.ds(own_row, 1)], spare_x, x_s)
    pltpu.make_async_copy(zsum.at[pl.ds(own_chip_row, 1)], own_z, z_r).start()
    pltpu.make_async_copy(vxall.at[pl.ds(own_row, 1)], own_x, x_r).start()

    out[...] = mm(nb, wop[...]).astype(BF)

    w_head = wo[pl.ds(plane * HEAD, HEAD)]
    c_head = ct[pl.ds(plane * PATCH, PATCH)]
    chosen = (iota((16, HEAD), 1) == 16 * lax.rem(ctx, 8) + iota((16, HEAD), 0)).astype(BF)
    c_rows = mm(chosen, c_head, NT).astype(BF)
    column = (iota((16, WIDTH), 1) == ctx * 16 + iota((16, WIDTH), 0)).astype(BF)
    embed_rows = mm(column, jnp.concatenate([we[...]] * HEADS, axis=0), NT).astype(BF)
    tall = jnp.concatenate([jnp.where(heads[h], embed_rows, jnp.zeros_like(embed_rows)) for h in range(HEADS)], axis=0)
    qkv_rows = wq[pl.ds(ctx * 16, 16)]
    long = jnp.concatenate(
        [
            jnp.concatenate(
                [qkv_rows[:, j * WIDTH + h * HEAD : j * WIDTH + (h + 1) * HEAD] for j in range(3)], axis=1
            )
            for h in range(HEADS)
        ],
        axis=0,
    )

    pltpu.make_async_copy(recv_z, recv_z, z_r).wait()
    fine = jnp.sum(recv_z[...], axis=0, keepdims=True)
    zrow[...] = fine
    high = fine.astype(BF)
    low = (fine - high.astype(F32)).astype(BF)
    yv = mm(high, w_head, NT) + mm(low, w_head, NT)
    own_zh = recv_zh.at[pl.ds(lax.rem(own_row, NCTX), 1)]
    for partner in plane_partners:
        push(zrow, own_zh, zh_s, zh_r, *partner)
    spare_copy(zrow, spare_zh, zh_s)
    pltpu.make_async_copy(zrow, own_zh, zh_r).start()
    pltpu.make_async_copy(recv_x, recv_x, x_r).wait()
    mixed = jnp.sum(recv_x[...], axis=0, keepdims=True)
    xs_sum = jnp.where(lane < 64, 0.0, mixed)
    yxrow[:, :HEAD] = yv - mm(mixed[:, :PATCH].astype(BF), c_head)
    yxrow[:, HEAD:] = xs_sum + pltpu.roll(xs_sum, 64, 1)
    own_yx = recv_yx.at[pl.ds(own_row, 1)]
    for partner in all_partners:
        push(yxrow, own_yx, yx_s, yx_r, *partner)
    spare_copy(yxrow, spare_yx, yx_s)
    pltpu.make_async_copy(yxrow, own_yx, yx_r).start()

    pltpu.make_async_copy(recv_zh, recv_zh, zh_r).wait()
    gout[...] = mm(c_rows, recv_zh[...].astype(BF))
    pltpu.make_async_copy(recv_yx, recv_yx, yx_r).wait()
    x_block = jnp.where(block, recv_yx[:, HEAD:], 0.0).astype(BF)
    yq = mm(x_block, bt[...])
    yk = mm(x_block, at[...], TN)
    ys = jnp.concatenate([yq, yk, recv_yx[:, :HEAD]], axis=1).astype(BF)
    wide = mm(tall, ys)
    for h in range(HEADS):
        for j in range(3):
            gqkv[:, j * WIDTH + h * HEAD : j * WIDTH + (h + 1) * HEAD] = wide[
                16 * h : 16 * h + 16, j * HEAD : (j + 1) * HEAD
            ]
    tops = mm(long, ys, NT)
    folded = jnp.zeros((16, HEAD), F32)
    for h in range(HEADS):
        folded = folded + jnp.where(heads[h], tops[16 * h : 16 * h + 16], 0.0)
    folded = folded + pltpu.roll(folded, 64, 1)
    folded = folded + pltpu.roll(folded, 32, 1)
    gemb[...] = folded[:, :PATCH]

    sent_mix = stage_mix.at[pl.ds(0, LB * (NMIX - 1))]
    pltpu.make_async_copy(sent_mix, sent_mix, mix_s).wait()
    for ref, sem in (
        (recv_g, g_s), (recv_r, r_s), (recv_m, m_s), (recv_s, s_s), (zpeer, zc_s), (recv_z, z_s), (recv_x, x_s), (recv_yx, yx_s), (recv_zh, zh_s)
    ):
        pltpu.make_async_copy(ref, ref, sem).wait()


def hand_on(*refs):
    copies = [pltpu.make_async_copy(refs[i], refs[4 + i], refs[8].at[i]) for i in range(4)]
    for copy in copies:
        copy.start()
    for copy in copies:
        copy.wait()


def shards(
    sources, source_ids, mix_weights, source_lengths, w_embed, w_qkv, w_out, forget, cotangent
):
    packed = sources.reshape(LOCAL_SOURCES, STEPS * PATCH // 128, 128).transpose(1, 0, 2)
    vm = pltpu.VMEM
    sm = pltpu.SMEM
    dma = pltpu.SemaphoreType.DMA
    results = pl.pallas_call(
        kernel,
        out_shape=tuple(vm(shape, kind) for shape, kind in RESULTS),
        in_specs=[pl.BlockSpec(memory_space=pl.ANY)] * 9,
        out_specs=(pl.BlockSpec(memory_space=pltpu.VMEM),) * 4,
        scratch_shapes=[
            vm((LOCAL_SOURCES, 64, 128), F32),
            sm((TERMS, LB * NMIX), jnp.int32),
            sm((TERMS, LB * NMIX), F32),
            sm((TERMS, LB * NMIX), jnp.int32),
            vm((PATCH, WIDTH), BF),
            vm((WIDTH, 3 * WIDTH), BF),
            vm((WIDTH, WIDTH), BF),
            vm((LB * HEADS, STEPS), F32),
            vm((ROWS, WIDTH), BF),
            vm((LB * NMIX, 64, 128), F32),
            vm((LB, NMIX, 64, 128), F32),
            vm((LB, HEAD), F32),
            vm((LB * ROW, HEAD), F32),
            vm((LB, HEAD), F32),
            vm((LB * PLANES, HEAD), F32),
            vm((LB * PATCH, HEAD), F32),
            vm((ROW, 8, HEAD), F32),
            vm((ROW, 8, HEAD), F32),
            vm((8, HEAD), F32),
            vm((PLANES, ROW, 8, HEAD), F32),
            vm((LB, STEPS, HEAD), F32),
            vm((LB, STEPS, HEAD), F32),
            vm((LB * HEADS, STEPS, STEPS), F32),
            vm((ROWS, HEAD), BF),
            vm((ROWS, HEAD), BF),
            vm((ROWS, HEAD), BF),
            vm((ROWS, HEAD), F32),
            vm((LB, PATCH, STEPS), BF),
            vm((ROWS, HEAD), F32),
            vm((LB, STEPS, HEAD), F32),
            vm((HEAD, HEAD), BF),
            vm((HEAD, HEAD), BF),
            vm((HEAD, HEAD), BF),
            vm((HEAD, WIDTH), BF),
            vm((HEAD, HEAD), BF),
            vm((2, HEAD, HEAD), BF),
            vm((HEAD, WIDTH), BF),
            vm((ROWS, HEAD), F32),
            vm((HEADS, 2, 16, WIDTH), F32),
            vm((HEADS, 16, WIDTH), F32),
            vm((NDEV // 2, WIDTH), F32),
            vm((NDEV // 2, WIDTH), F32),
            vm((NDEV, HEAD), F32),
            vm((NDEV, HEAD), F32),
            vm((1, WIDTH), F32),
            vm((NCTX, WIDTH), F32),
            vm((1, 2 * HEAD), F32),
            vm((NDEV, 2 * HEAD), F32),
            vm((LB, HEAD), F32),
            vm((LB, HEAD), F32),
            vm((8, HEAD), F32),
            vm((8, HEAD), F32),
            vm((1, WIDTH), F32),
            vm((1, HEAD), F32),
            vm((1, 2 * HEAD), F32),
            vm((1, WIDTH), F32),
            dma((13,)),
        ]
        + [dma(()), dma((LB,))]
        + [dma(())] * 18,
        compiler_params=pltpu.CompilerParams(collective_id=0, has_side_effects=True, vmem_limit_bytes=60 << 20),
        name="whole_step",
    )(
        packed, source_ids.T, mix_weights.T, source_lengths.T, w_embed.T, w_qkv, w_out, forget,
        cotangent.reshape(ROWS, WIDTH),
    )
    output, grad_qkv, grad_out, grad_embed = pl.pallas_call(
        hand_on,
        out_shape=tuple(jax.ShapeDtypeStruct(shape, kind) for shape, kind in RESULTS),
        in_specs=[pl.BlockSpec(memory_space=pltpu.VMEM)] * 4,
        out_specs=(pl.BlockSpec(memory_space=pl.ANY),) * 4,
        scratch_shapes=[dma((4,))],
        name="hand_on",
    )(*[pltpu.with_memory_space_constraint(result, pltpu.VMEM) for result in results])
    return (output.reshape(LB, STEPS, WIDTH), grad_qkv, grad_out, grad_embed)


def solution(mesh):
    placed = (
        P("mix", "ctx"),
        P(),
        P(),
        P(),
        P(),
        P(),
        P(),
        P("mix", None, "ctx"),
        P("mix", "ctx", None),
    )
    return jax.shard_map(
        shards,
        mesh=mesh,
        in_specs=placed,
        out_specs=(P("mix", "ctx", None), P("ctx", None), P("ctx", None), P("ctx", None)),
        check_vma=False,
    )
```

```python
import jax
import jax.numpy as jnp
from jax import lax
from jax.experimental import pallas as pl
from jax.experimental.pallas import tpu as pltpu
from jax.sharding import PartitionSpec as P

EPS = 1e-06
BF = jnp.bfloat16
F32 = jnp.float32
MESH = pl.DeviceIdType.MESH
NCTX = 32
NMIX = 4
NDEV = 128
ROW = 8
PLANES = 4
LB = 2
HEADS = 4
PATCH = 32
STEPS = 256
ROWS = LB * STEPS
HEAD = 128
WIDTH = 512
LOCAL_SOURCES = 4
TERMS = 3
RESULTS = (((ROWS, WIDTH), BF), ((16, 3 * WIDTH), F32), ((16, WIDTH), F32), ((16, PATCH), F32))


def mm(left, right, dims=((1,), (0,))):
    return lax.dot_general(left, right, (dims, ((), ())), preferred_element_type=F32)


NT = ((1,), (1,))
TN = ((0,), (0,))


def mm_exact(left, right, dims):
    return lax.dot_general(
        left, right, (dims, ((), ())), precision=lax.Precision.HIGHEST, preferred_element_type=F32
    )


def far(d):
    return min(d, 4 - d)


CTX_STEPS = sorted(
    ((y, x, c) for y in range(4) for x in range(4) for c in range(2) if y or x or c),
    key=lambda o: -(3 * far(o[0]) + 3 * far(o[1]) + o[2]),
)
ALL_STEPS = sorted(
    ((y, x, c, z) for y in range(4) for x in range(4) for c in range(2) for z in range(4) if y or x or c or z),
    key=lambda o: -(3 * far(o[0]) + 3 * far(o[1]) + o[2] + 3 * far(o[3])),
)


def iota(shape, axis):
    return lax.broadcasted_iota(jnp.int32, shape, axis)


def kernel(
    src_hbm, ids_hbm, wts_hbm, lens_hbm, we_hbm, wq_hbm, wo_hbm, forget_hbm, cot_hbm,
    out, gqkv, gout, gemb,
    src, ids, wts, lens, we, wq, wo, forget, cot,
    stage_mix, recv_mix, glast, recv_g, row_gate, recv_r, m_local, recv_m, stage_s, stage_t, recv_s,
    rise, fade, tall_rows, decay, m4, mgs, mgp, u_ref, mt, y_ref, gcol, at, bt, ct, ctbig, gram, kk, wop, y0,
    zmat, zpeer, zsum, recv_z, vxall, recv_x, zrow, recv_zh, yxrow, recv_yx,
    spare_g, spare_r, spare_m, spare_s, spare_z, spare_x, spare_yx, spare_zh,
    in_sem, mix_s, mix_r, g_s, g_r, r_s, r_r, m_s, m_r, s_s, s_r, zc_s, zc_r, z_s, z_r, x_s, x_r, zh_s, zh_r, yx_s, yx_r,
):
    ctx = lax.axis_index("ctx")
    mix = lax.axis_index("mix")
    me = ctx * NMIX + mix
    plane = ctx // 8

    moves = [
        (ids_hbm, ids), (wts_hbm, wts), (lens_hbm, lens),
        (we_hbm, we), (wq_hbm, wq), (wo_hbm, wo), (cot_hbm, cot),
    ]
    moves = [(src_hbm.at[:, s], src.at[s]) for s in range(LOCAL_SOURCES)] + moves
    moves += [(forget_hbm.at[b], forget.at[pl.ds(b * HEADS, HEADS)]) for b in range(LB)]
    copies = [pltpu.make_async_copy(a, b, in_sem.at[i]) for i, (a, b) in enumerate(moves)]
    part_loads, weight_loads, cot_load, gate_loads = copies[:7], copies[7:10], copies[10], copies[11:]
    for copy in part_loads:
        copy.start()

    ys = [lax.rem(ctx // 8 + d, 4) * 8 for d in range(4)]
    xs = [lax.rem(ctx // 2 + d, 4) * 2 for d in range(4)]
    cs = [lax.rem(ctx + d, 2) for d in range(2)]
    zs = [lax.rem(mix + d, NMIX) for d in range(NMIX)]
    all_partners = [(ys[y] + xs[x] + cs[c], zs[z]) for y, x, c, z in ALL_STEPS]
    plane_partners = [(ys[y] + xs[x] + cs[c], zs[z]) for y, x, c, z in ALL_STEPS if y == 0]

    place_x = lax.rem(ctx, 8)
    all_rows = [(ys[y] * 4 + cs[c] * 16 + xs[x] * 2 + zs[z]) for y, x, c, z in ALL_STEPS]
    own_row = ys[0] * 4 + cs[0] * 16 + xs[0] * 2 + zs[0]
    chip_rows = [ys[y] * 2 + xs[x] * 2 + zs[z] for y, x, c, z in ALL_STEPS]
    own_chip_row = ys[0] * 2 + xs[0] * 2 + zs[0]
    row_partners = [(xs[x] + cs[c]) for y, x, c in CTX_STEPS if y == 0]

    barrier = pltpu.get_barrier_semaphore()
    for level in zs[1:]:
        pl.semaphore_signal(barrier, inc=1, device_id=(ctx, level), device_id_type=MESH)
    for other in row_partners:
        pl.semaphore_signal(barrier, inc=1, device_id=(ys[0] + other, mix), device_id_type=MESH)
    for base in ys[1:]:
        pl.semaphore_signal(barrier, inc=1, device_id=(base + place_x, mix), device_id_type=MESH)

    for copy in gate_loads + weight_loads + [cot_load]:
        copy.start()

    for load in part_loads:
        load.wait()
    place = ctx * STEPS + 4 * iota((64, 128), 0) + iota((64, 128), 1) // PATCH
    for b in range(LB * NMIX):
        part = jnp.zeros((64, 128), F32)
        for j in range(TERMS):
            slot = ids[j, b] - mix * LOCAL_SOURCES
            held = jnp.clip(slot, 0, LOCAL_SOURCES - 1)
            weight = jnp.where(slot == held, wts[j, b], 0.0)
            part = part + jnp.where(place < lens[j, b], weight, 0.0) * src[held]
        stage_mix[b] = part

    pl.semaphore_wait(barrier, NMIX - 1 + ROW - 1 + PLANES - 1)

    for b in range(LB):
        landing = recv_mix.at[b, mix]
        for level in (zs[2], zs[1], zs[3]):
            pltpu.make_async_remote_copy(
                stage_mix.at[LB * level + b], landing, mix_s, mix_r.at[b],
                device_id=(ctx, level), device_id_type=MESH,
            ).start()
        pltpu.make_async_copy(stage_mix.at[LB * mix + b], landing, mix_r.at[b]).start()

    def spare_copy(part, spare, send):
        pltpu.make_async_copy(part, spare, send).start()

    def push(source, target, send, recv, other, level):
        pltpu.make_async_remote_copy(
            source, target, send, recv, device_id=(other, level), device_id_type=MESH
        ).start()

    for load in gate_loads:
        load.wait()
    growth = jnp.log1p(forget[...] - 1.0)
    lanes = iota((LB * HEADS, STEPS), 1)
    for k in (1, 2, 4, 8, 16, 32, 64, 128):
        growth = growth + jnp.where(lanes >= k, pltpu.roll(growth, k, 1), 0.0)
    for b in range(LB):
        col = jnp.concatenate(
            [
                jnp.broadcast_to(growth[b * HEADS + h : b * HEADS + h + 1], (PATCH, STEPS))
                for h in range(HEADS)
            ],
            axis=0,
        ).T
        gcol[b] = col
        last = col[STEPS - 1 : STEPS]
        glast[b : b + 1] = last
        rise[b] = jnp.exp(col)
        fade[b] = jnp.exp(last - col)

    own_g = recv_g.at[pl.ds(LB * place_x, LB)]
    for other in row_partners:
        push(glast, own_g, g_s, g_r, ys[0] + other, mix)
    pltpu.make_async_copy(glast, own_g, g_r).start()
    spare_copy(glast, spare_g, g_s)

    for load in weight_loads:
        load.wait()
    wt = mm(we[...], wq[...]).astype(BF)
    lane = iota((1, HEAD), 1)
    block = iota((HEAD, HEAD), 0) // PATCH == iota((HEAD, HEAD), 1) // PATCH
    heads = [lane // PATCH == h for h in range(HEADS)]
    for h in range(HEADS):
        rows = pl.ds(h * PATCH, PATCH)
        at[rows] = wt[:, h * HEAD : (h + 1) * HEAD]
        bt[rows] = wt[:, WIDTH + h * HEAD : WIDTH + (h + 1) * HEAD]
        piece = wt[:, 2 * WIDTH + h * HEAD : 2 * WIDTH + (h + 1) * HEAD]
        ct[rows] = piece
        for k in range(HEADS):
            ctbig[rows, k * HEAD : (k + 1) * HEAD] = piece if k == h else jnp.zeros_like(piece)
    gram[...] = jnp.where(block, mm(at[...], bt[...], NT), 0.0).astype(BF)
    square = jnp.where(block, mm(ct[...], ct[...], NT), 0.0)
    kk[0] = square.astype(BF)
    kk[1] = (square - kk[0].astype(F32)).astype(BF)
    wop[...] = mm(ctbig[...], wo[...]).astype(BF)
    causal = iota((STEPS, STEPS), 0) >= iota((STEPS, STEPS), 1)
    for b in range(LB):
        for h in range(HEADS):
            diff = gcol[b][:, h * PATCH : h * PATCH + 1] - growth[b * HEADS + h : b * HEADS + h + 1]
            decay[b * HEADS + h] = jnp.where(causal, jnp.exp(diff), 0.0)

    pltpu.make_async_copy(recv_g, recv_g, g_r).wait()
    gates = [recv_g[LB * q : LB * q + LB] for q in range(ROW)]
    inner = jnp.zeros((LB, HEAD), F32)
    whole = jnp.zeros((LB, HEAD), F32)
    for q in range(ROW):
        inner = inner + jnp.where(q < place_x, gates[q], 0.0)
        whole = whole + gates[q]
    row_gate[...] = whole
    own_r = recv_r.at[pl.ds(LB * plane, LB)]
    for base in ys[1:]:
        push(row_gate, own_r, r_s, r_r, base + place_x, mix)
    pltpu.make_async_copy(row_gate, own_r, r_r).start()
    spare_copy(row_gate, spare_r, r_s)

    spread = (lax.rem(iota((HEAD, HEAD), 0), PATCH) == lax.rem(iota((HEAD, HEAD), 1), PATCH)).astype(BF)
    mine = lax.rem(iota((STEPS, HEAD), 0), 4) == iota((STEPS, HEAD), 1) // PATCH
    for b in range(LB):
        pltpu.make_async_copy(recv_mix.at[b], recv_mix.at[b], mix_r.at[b]).wait()
        packed = ((recv_mix[b, 0] + recv_mix[b, 1]) + (recv_mix[b, 2] + recv_mix[b, 3]))
        for k in range(4):
            tall_rows[b, pl.ds(k, 64, stride=4)] = packed
        lone = jnp.where(mine, tall_rows[b], 0.0).astype(BF)
        rows = mm(lone, spread)
        m4[pl.ds(b * STEPS, STEPS)] = rows.astype(BF)
        faded = (rows * fade[b]).astype(BF)
        m_local[pl.ds(b * PATCH, PATCH)] = mm(rows.astype(BF), faded, TN)[:PATCH]
    own_m = recv_m.at[place_x]
    for other in row_partners:
        push(m_local.at[pl.ds(8 * other, 8)], own_m, m_s, m_r, ys[0] + other, mix)
    mine_m = m_local.at[pl.ds(8 * place_x, 8)]
    pltpu.make_async_copy(mine_m, own_m, m_r).start()
    spare_copy(mine_m, spare_m, m_s)

    def scores(b):
        rows = pl.ds(b * STEPS, STEPS)
        mg = mm(m4[rows], gram[...])
        mgp[rows] = mg.astype(BF)
        mgs[rows] = (mg * rise[b]).astype(BF)

    def inside(b, some, total):
        rows = pl.ds(b * STEPS, STEPS)
        mb, mgb = m4[rows], mgp[rows]
        for h in some:
            score = mm(jnp.where(heads[h], mgb, jnp.zeros_like(mgb)), mb, NT)
            score = (score * decay[b * HEADS + h]).astype(BF)
            part = mm(score, jnp.where(heads[h], mb, jnp.zeros_like(mb)))
            total = part if total is None else total + part
        u_ref[rows] = total

    scores(0)
    inside(0, (0, 1), None)

    pltpu.make_async_copy(recv_m, recv_m, m_r).wait()
    own_b = place_x // (ROW // LB)
    state = jnp.zeros((8, HEAD), F32)
    for q in range(ROW):
        stage_s[q] = state
        state = jnp.exp(recv_g[pl.ds(LB * q + own_b, 1)]) * state + recv_m[q]
    stage_t[...] = state
    own_s = recv_s.at[plane, place_x]
    for y, x, c in CTX_STEPS:
        other = xs[x] + cs[c]
        push(stage_s.at[other] if y == 0 else stage_t, own_s, s_s, s_r, ys[y] + other, mix)
    pltpu.make_async_copy(stage_s.at[place_x], own_s, s_r).start()
    spare_copy(stage_t, spare_s, s_s)

    inside(0, (2, 3), u_ref[pl.ds(0, STEPS)])
    scores(1)
    inside(1, range(HEADS), None)
    for b in range(LB):
        mt[b] = m4[pl.ds(b * STEPS, STEPS)].astype(F32).T[:PATCH].astype(BF)
    cot_load.wait()
    y0[...] = mm(cot[...], wop[...], NT)
    pltpu.make_async_copy(recv_r, recv_r, r_r).wait()
    factors = []
    reach = inner
    for back in range(PLANES):
        factors.append(reach)
        if back < PLANES - 1:
            reach = reach + recv_r[pl.ds(LB * jnp.maximum(plane - 1 - back, 0), LB)]
    pltpu.make_async_copy(recv_s, recv_s, s_r).wait()

    memory = []
    for b in range(LB):
        part = recv_s[plane, b * 4 : b * 4 + 4].reshape(PATCH, HEAD)
        for back in range(1, PLANES):
            earlier = recv_s[jnp.maximum(plane - back, 0), b * 4 : b * 4 + 4].reshape(PATCH, HEAD)
            weight = jnp.where(plane >= back, jnp.exp(factors[back - 1][b : b + 1]), 0.0)
            part = part + weight * earlier
        memory.append(
            jnp.where(block, jnp.concatenate([part] * HEADS, axis=0), 0.0).astype(BF)
        )
        rows = pl.ds(b * STEPS, STEPS)
        u_ref[rows] = u_ref[rows] + mm(mgs[rows], memory[b])
    u = u_ref[...]
    ub = u.astype(BF)
    ku = mm(ub, kk[0]) + mm(ub, kk[1])
    ones = block.astype(BF)
    square = ub.astype(F32) * ku
    high = square.astype(BF)
    low = (square - high.astype(F32)).astype(BF)
    square = (mm(high, ones) + mm(low, ones)) * (1.0 / HEAD)
    inv = lax.rsqrt(jnp.maximum(square, 0.0) + EPS)
    n = u * inv
    nb = n.astype(BF)
    dots = mm((y0[...] * u).astype(BF), ones) * (1.0 / HEAD)
    zmat[...] = mm(nb, cot[...], TN).reshape(HEADS, 2, 16, WIDTH)
    push(zmat.at[:, cs[1]], zpeer, zc_s, zc_r, ys[0] + xs[0] + cs[1], mix)

    drift = inv * (inv * dots)
    y = inv * (y0[...] - drift * ku)
    y_ref[...] = y
    inside_x = jnp.zeros((HEAD, HEAD), F32)
    before_x = jnp.zeros((HEAD, HEAD), F32)
    for b in range(LB):
        rows = pl.ds(b * STEPS, STEPS)
        mb = m4[rows]
        yb = y_ref[rows]
        yh = yb.astype(BF)
        stacked = jnp.concatenate([jnp.where(heads[h], yh, jnp.zeros_like(yh)) for h in range(HEADS)], axis=0)
        left = mm(stacked, mb, NT)
        parts = []
        for h in range(HEADS):
            one = (left[h * STEPS : (h + 1) * STEPS] * decay[b * HEADS + h]).astype(BF)
            parts.append(mm(mt[b], one).astype(BF))
        inside_x = inside_x + mm(jnp.concatenate(parts, axis=0), mb)
        risen = mm(mt[b], (yb * rise[b]).astype(BF))
        risen = jnp.where(block, jnp.concatenate([risen] * HEADS, axis=0), 0.0).astype(BF)
        before_x = before_x + mm(risen, memory[b])

    def repeat(square_block):
        kept = jnp.where(block, square_block, 0.0)
        kept = kept + pltpu.roll(kept, 64, 1)
        return kept + pltpu.roll(kept, 32, 1)

    v_rows = repeat(mm((n * (inv * dots)).astype(BF), nb, TN))
    x_rows = inside_x + repeat(before_x)
    vxall[...] = jnp.where(lane < 64, v_rows, x_rows)
    own_z = recv_z.at[pl.ds(own_chip_row, 1)]
    own_x = recv_x.at[pl.ds(own_row, 1)]
    for row, partner in zip(all_rows[:40], all_partners):
        push(vxall.at[pl.ds(row, 1)], own_x, x_s, x_r, *partner)
    pltpu.make_async_copy(zpeer, zpeer, zc_r).wait()
    zsum[...] = (zmat[:, cs[0]] + zpeer[...]).reshape(NDEV // 2, WIDTH)
    for n, (step, row, chip_row, partner) in enumerate(zip(ALL_STEPS, all_rows, chip_rows, all_partners)):
        if step[2] == 0:
            push(zsum.at[pl.ds(chip_row, 1)], own_z, z_s, z_r, *partner)
        if n >= 40:
            push(vxall.at[pl.ds(row, 1)], own_x, x_s, x_r, *partner)
    spare_copy(zsum.at[pl.ds(own_chip_row, 1)], spare_z, z_s)
    spare_copy(vxall.at[pl.ds(own_row, 1)], spare_x, x_s)
    pltpu.make_async_copy(zsum.at[pl.ds(own_chip_row, 1)], own_z, z_r).start()
    pltpu.make_async_copy(vxall.at[pl.ds(own_row, 1)], own_x, x_r).start()

    out[...] = mm(nb, wop[...]).astype(BF)

    w_head = wo[pl.ds(plane * HEAD, HEAD)]
    c_head = ct[pl.ds(plane * PATCH, PATCH)]
    chosen = (iota((16, HEAD), 1) == 16 * lax.rem(ctx, 8) + iota((16, HEAD), 0)).astype(BF)
    c_rows = mm(chosen, c_head, NT).astype(BF)
    column = (iota((16, WIDTH), 1) == ctx * 16 + iota((16, WIDTH), 0)).astype(BF)
    embed_rows = mm(column, jnp.concatenate([we[...]] * HEADS, axis=0), NT).astype(BF)
    tall = jnp.concatenate([jnp.where(heads[h], embed_rows, jnp.zeros_like(embed_rows)) for h in range(HEADS)], axis=0)
    qkv_rows = wq[pl.ds(ctx * 16, 16)]
    long = jnp.concatenate(
        [
            jnp.concatenate(
                [qkv_rows[:, j * WIDTH + h * HEAD : j * WIDTH + (h + 1) * HEAD] for j in range(3)], axis=1
            )
            for h in range(HEADS)
        ],
        axis=0,
    )

    pltpu.make_async_copy(recv_z, recv_z, z_r).wait()
    fine = jnp.sum(recv_z[...], axis=0, keepdims=True)
    zrow[...] = fine
    high = fine.astype(BF)
    low = (fine - high.astype(F32)).astype(BF)
    yv = mm(high, w_head, NT) + mm(low, w_head, NT)
    own_zh = recv_zh.at[pl.ds(lax.rem(own_row, NCTX), 1)]
    for partner in plane_partners:
        push(zrow, own_zh, zh_s, zh_r, *partner)
    spare_copy(zrow, spare_zh, zh_s)
    pltpu.make_async_copy(zrow, own_zh, zh_r).start()
    pltpu.make_async_copy(recv_x, recv_x, x_r).wait()
    mixed = jnp.sum(recv_x[...], axis=0, keepdims=True)
    xs_sum = jnp.where(lane < 64, 0.0, mixed)
    yxrow[:, :HEAD] = yv - mm(mixed[:, :PATCH].astype(BF), c_head)
    yxrow[:, HEAD:] = xs_sum + pltpu.roll(xs_sum, 64, 1)
    own_yx = recv_yx.at[pl.ds(own_row, 1)]
    for partner in all_partners:
        push(yxrow, own_yx, yx_s, yx_r, *partner)
    spare_copy(yxrow, spare_yx, yx_s)
    pltpu.make_async_copy(yxrow, own_yx, yx_r).start()

    pltpu.make_async_copy(recv_zh, recv_zh, zh_r).wait()
    gout[...] = mm(c_rows, recv_zh[...].astype(BF))
    pltpu.make_async_copy(recv_yx, recv_yx, yx_r).wait()
    x_block = jnp.where(block, recv_yx[:, HEAD:], 0.0).astype(BF)
    yq = mm(x_block, bt[...])
    yk = mm(x_block, at[...], TN)
    ys = jnp.concatenate([yq, yk, recv_yx[:, :HEAD]], axis=1).astype(BF)
    wide = mm(tall, ys)
    for h in range(HEADS):
        for j in range(3):
            gqkv[:, j * WIDTH + h * HEAD : j * WIDTH + (h + 1) * HEAD] = wide[
                16 * h : 16 * h + 16, j * HEAD : (j + 1) * HEAD
            ]
    tops = mm(long, ys, NT)
    folded = jnp.zeros((16, HEAD), F32)
    for h in range(HEADS):
        folded = folded + jnp.where(heads[h], tops[16 * h : 16 * h + 16], 0.0)
    folded = folded + pltpu.roll(folded, 64, 1)
    folded = folded + pltpu.roll(folded, 32, 1)
    gemb[...] = folded[:, :PATCH]

    sent_mix = stage_mix.at[pl.ds(0, LB * (NMIX - 1))]
    pltpu.make_async_copy(sent_mix, sent_mix, mix_s).wait()
    for ref, sem in (
        (recv_g, g_s), (recv_r, r_s), (recv_m, m_s), (recv_s, s_s), (zpeer, zc_s), (recv_z, z_s), (recv_x, x_s), (recv_yx, yx_s), (recv_zh, zh_s)
    ):
        pltpu.make_async_copy(ref, ref, sem).wait()


def hand_on(*refs):
    copies = [pltpu.make_async_copy(refs[i], refs[4 + i], refs[8].at[i]) for i in range(4)]
    for copy in copies:
        copy.start()
    for copy in copies:
        copy.wait()


def shards(
    sources, source_ids, mix_weights, source_lengths, w_embed, w_qkv, w_out, forget, cotangent
):
    packed = sources.reshape(LOCAL_SOURCES, STEPS * PATCH // 128, 128).transpose(1, 0, 2)
    vm = pltpu.VMEM
    sm = pltpu.SMEM
    dma = pltpu.SemaphoreType.DMA
    results = pl.pallas_call(
        kernel,
        out_shape=tuple(vm(shape, kind) for shape, kind in RESULTS),
        in_specs=[pl.BlockSpec(memory_space=pl.ANY)] * 9,
        out_specs=(pl.BlockSpec(memory_space=pltpu.VMEM),) * 4,
        scratch_shapes=[
            vm((LOCAL_SOURCES, 64, 128), F32),
            sm((TERMS, LB * NMIX), jnp.int32),
            sm((TERMS, LB * NMIX), F32),
            sm((TERMS, LB * NMIX), jnp.int32),
            vm((PATCH, WIDTH), BF),
            vm((WIDTH, 3 * WIDTH), BF),
            vm((WIDTH, WIDTH), BF),
            vm((LB * HEADS, STEPS), F32),
            vm((ROWS, WIDTH), BF),
            vm((LB * NMIX, 64, 128), F32),
            vm((LB, NMIX, 64, 128), F32),
            vm((LB, HEAD), F32),
            vm((LB * ROW, HEAD), F32),
            vm((LB, HEAD), F32),
            vm((LB * PLANES, HEAD), F32),
            vm((LB * PATCH, HEAD), F32),
            vm((ROW, 8, HEAD), F32),
            vm((ROW, 8, HEAD), F32),
            vm((8, HEAD), F32),
            vm((PLANES, ROW, 8, HEAD), F32),
            vm((LB, STEPS, HEAD), F32),
            vm((LB, STEPS, HEAD), F32),
            vm((LB, STEPS, HEAD), F32),
            vm((LB * HEADS, STEPS, STEPS), F32),
            vm((ROWS, HEAD), BF),
            vm((ROWS, HEAD), BF),
            vm((ROWS, HEAD), BF),
            vm((ROWS, HEAD), F32),
            vm((LB, PATCH, STEPS), BF),
            vm((ROWS, HEAD), F32),
            vm((LB, STEPS, HEAD), F32),
            vm((HEAD, HEAD), BF),
            vm((HEAD, HEAD), BF),
            vm((HEAD, HEAD), BF),
            vm((HEAD, WIDTH), BF),
            vm((HEAD, HEAD), BF),
            vm((2, HEAD, HEAD), BF),
            vm((HEAD, WIDTH), BF),
            vm((ROWS, HEAD), F32),
            vm((HEADS, 2, 16, WIDTH), F32),
            vm((HEADS, 16, WIDTH), F32),
            vm((NDEV // 2, WIDTH), F32),
            vm((NDEV // 2, WIDTH), F32),
            vm((NDEV, HEAD), F32),
            vm((NDEV, HEAD), F32),
            vm((1, WIDTH), F32),
            vm((NCTX, WIDTH), F32),
            vm((1, 2 * HEAD), F32),
            vm((NDEV, 2 * HEAD), F32),
            vm((LB, HEAD), F32),
            vm((LB, HEAD), F32),
            vm((8, HEAD), F32),
            vm((8, HEAD), F32),
            vm((1, WIDTH), F32),
            vm((1, HEAD), F32),
            vm((1, 2 * HEAD), F32),
            vm((1, WIDTH), F32),
            dma((13,)),
        ]
        + [dma(()), dma((LB,))]
        + [dma(())] * 18,
        compiler_params=pltpu.CompilerParams(collective_id=0, has_side_effects=True, vmem_limit_bytes=60 << 20),
        name="whole_step",
    )(
        packed, source_ids.T, mix_weights.T, source_lengths.T, w_embed.T, w_qkv, w_out, forget,
        cotangent.reshape(ROWS, WIDTH),
    )
    output, grad_qkv, grad_out, grad_embed = pl.pallas_call(
        hand_on,
        out_shape=tuple(jax.ShapeDtypeStruct(shape, kind) for shape, kind in RESULTS),
        in_specs=[pl.BlockSpec(memory_space=pltpu.VMEM)] * 4,
        out_specs=(pl.BlockSpec(memory_space=pl.ANY),) * 4,
        scratch_shapes=[dma((4,))],
        name="hand_on",
    )(*[pltpu.with_memory_space_constraint(result, pltpu.VMEM) for result in results])
    return (output.reshape(LB, STEPS, WIDTH), grad_qkv, grad_out, grad_embed)


def solution(mesh):
    placed = (
        P("mix", "ctx"),
        P(),
        P(),
        P(),
        P(),
        P(),
        P(),
        P("mix", None, "ctx"),
        P("mix", "ctx", None),
    )
    return jax.shard_map(
        shards,
        mesh=mesh,
        in_specs=placed,
        out_specs=(P("mix", "ctx", None), P("ctx", None), P("ctx", None), P("ctx", None)),
        check_vma=False,
    )
```
